32 devices in a mesh: azi: 8 (over z, core), rad: 4 (over y, x).
Axes of the slice: x: 2, y: 2, z: 4, core: 2. Of those that a mesh axis runs over, the one named last changes fastest.
Arguments:
- trace_azimuth: bfloat16 [80, 256, 512], P(None, 'azi', 'rad'), may hold values from -6 to 6
- trace_radial: bfloat16 [80, 256, 512], P(None, 'azi', 'rad'), may hold values from -6 to 6
- state: bfloat16 [1080, 256, 512], P(None, 'azi', 'rad'), may hold values from -6 to 6
- jacobian: bfloat16 [1080, 1080], replicated, may hold values from -0.1875 to 0.1875
- lift_map: bfloat16 [1080, 320], replicated, may hold values from -0.3125 to 0.3125
- order: int32 [256, 512], P('azi', 'rad'), may hold values from 4 to 5, as said below
- patch: int32 [256, 512], P('azi', 'rad'), may hold values from 0 to 1535, as said below
Outputs:
- indicator: float32 [1536, 90], P(('azi', 'rad'))
The draws below stay inside these ranges and needn't reach their ends.
Inputs may be any that keep to these rules, and one draw needn't show every extreme that they name: Each device's block of 32 x 128 elements holds 384 to 1536 elements of order 5, and some device exactly 1536; all others have order 4. Each patch is a contiguous run of elements along the radius within a band of 16 azimuthal element rows; runs may cross the radial border between devices. The elements of one device lie in at most 50 patches, of which at most 25 belong to any one owner; both bounds are reached on some device in every draw.
All inputs are finite; a program needn't handle non-finite values.
Results may differ from the reference program's by a relative error of at most 0.0003.
Values may be sent and summed in bfloat16 or wider, within the bound.
A program may use at most 128 MiB of HBM per device.

```python
import jax
import jax.numpy as jnp
from jax import lax

DEG = 6
MODES = 216
KMAX = 1080
FACE = 80
GROUPS = 90
EA = 32
ER = 128
PATCH_DEV = 48
C5 = 1536
NAZ_EL = 256
NRD_EL = 512
NP = 1536


def draw_order(key, part):
    blocks = NAZ_EL // EA * (NRD_EL // ER)
    elements = EA * ER
    key_count, key_top, key_perm = jax.random.split(jax.random.fold_in(key, 17), 3)
    counts = jax.random.randint(key_count, (blocks,), C5 // 4, C5 + 1)
    top_block = jax.random.randint(key_top, (), 0, blocks)
    counts = jnp.where(jnp.arange(blocks) == top_block, C5, counts)
    ranks = jax.vmap(lambda one_key: jax.random.permutation(one_key, elements))(jax.random.split(key_perm, blocks))
    values = jnp.where(ranks < counts[:, None], 5, 4).astype(jnp.int32)
    values = values.reshape(NAZ_EL // EA, NRD_EL // ER, EA, ER).transpose(0, 2, 1, 3)
    return values.reshape(NAZ_EL, NRD_EL)


def draw_patch(key, part):
    radial_devices = NRD_EL // ER
    all_devices = NAZ_EL // EA * radial_devices
    bands = NAZ_EL // (EA // 2)
    ranges = radial_devices + 1
    half = ER // 2
    spots = half - 1
    quarter = PATCH_DEV // 4
    per_band = radial_devices * PATCH_DEV // 2
    key_first, key_second, key_owner = jax.random.split(jax.random.fold_in(key, 29), 3)
    first_rank = jax.vmap(lambda one_key: jax.random.permutation(one_key, spots))(jax.random.split(key_first, bands * ranges)).reshape(bands, ranges, spots)
    second_rank = jax.vmap(lambda one_key: jax.random.permutation(one_key, spots))(jax.random.split(key_second, bands * ranges)).reshape(bands, ranges, spots)
    range_index = jnp.arange(ranges, dtype=jnp.int32)[None, :, None]
    first_flags = (first_rank < quarter - 1).astype(jnp.int32)
    second_limit = jnp.where(range_index == 0, quarter - 1, quarter)
    second_flags = (second_rank < second_limit).astype(jnp.int32)
    lead = jnp.ones((bands, ranges, 1), jnp.int32)
    middle = jnp.where(range_index == 0, 1, 0) * jnp.ones((bands, ranges, 1), jnp.int32)
    flags = jnp.concatenate([lead, first_flags, middle, second_flags], axis=2).reshape(bands, ranges * ER)
    flags = flags[:, half:half + NRD_EL]
    tile = jnp.cumsum(flags, axis=1) - 1
    tile = tile + jnp.arange(bands, dtype=jnp.int32)[:, None] * per_band
    owner_map = jax.random.permutation(key_owner, all_devices).astype(jnp.int32)
    span = tile // PATCH_DEV
    owner = jnp.sum((span[:, :, None] == jnp.arange(all_devices, dtype=jnp.int32)[None, None, :]).astype(jnp.int32) * owner_map[None, None, :], axis=2)
    values = owner * PATCH_DEV + tile % PATCH_DEV
    values = jnp.repeat(values, EA // 2, axis=0)
    return values.astype(jnp.int32)


def block_scale(rng, shape, cuts, least, largest):
    factor_of = 1.0
    for position, parts in cuts:
        draws = jax.random.uniform(jax.random.fold_in(jax.random.fold_in(rng, 6), position), (parts,), jnp.float32, least / len(cuts), largest / len(cuts))
        factor_of = factor_of * jnp.repeat(jnp.exp(draws), shape[position] // parts).reshape((-1,) + (1,) * (len(shape) - 1 - position))
    return factor_of


def scatter_about(rng, extent, scale, most, cuts=(), held_as=jnp.bfloat16):
    values = jax.random.normal(rng, extent, jnp.float32) * scale
    if len(cuts) > 0:
        values = block_scale(rng, extent, cuts, -0.22, 0.18) * values
    return jnp.clip(values, min=-most, max=most).astype(held_as)


def setup_inputs(seed: int = 0) -> dict:
    arg_keys = jax.random.split(jax.random.key(seed), 8)
    trace_azimuth = scatter_about(arg_keys[0], (FACE, NAZ_EL, NRD_EL), 1.0, 6.0, ((1, 8), (2, 4)))
    trace_radial = scatter_about(arg_keys[1], (FACE, NAZ_EL, NRD_EL), 1.0, 6.0, ((1, 8), (2, 4)))
    state = scatter_about(arg_keys[2], (KMAX, NAZ_EL, NRD_EL), 1.0, 6.0, ((1, 8), (2, 4)))
    jacobian = scatter_about(arg_keys[3], (KMAX, KMAX), KMAX ** -0.5, 0.1875)
    lift_map = scatter_about(arg_keys[4], (KMAX, 4 * FACE), (4 * FACE) ** -0.5, 0.3125)
    order = draw_order(jax.random.fold_in(arg_keys[7], 71), 0)
    patch = draw_patch(jax.random.fold_in(arg_keys[7], 71), 0)
    return dict(trace_azimuth=trace_azimuth, trace_radial=trace_radial, state=state, jacobian=jacobian, lift_map=lift_map, order=order, patch=patch)


def mode_tables():
    mode_index = jnp.arange(KMAX, dtype=jnp.int32)
    variable = mode_index // MODES
    inside = mode_index % MODES
    degrees = [inside // (DEG * DEG), (inside // DEG) % DEG, inside % DEG]
    lower_modes = jnp.maximum(jnp.maximum(degrees[0], degrees[1]), degrees[2]) <= DEG - 2
    group_index = jnp.arange(GROUPS, dtype=jnp.int32)
    group_table = jnp.zeros((GROUPS, KMAX), jnp.float32)
    for direction in range(3):
        target = variable * 3 * DEG + direction * DEG + degrees[direction]
        group_table = group_table + (group_index[:, None] == target[None, :]).astype(jnp.float32)
    return lower_modes, group_table


def reference(trace_azimuth, trace_radial, state, jacobian, lift_map, order, patch):
    behind_azimuth = jnp.roll(trace_azimuth, 1, axis=1)
    behind_radial = jnp.concatenate([jnp.zeros_like(trace_radial[:, :, :1]), trace_radial[:, :, :-1]], axis=2)
    lower_modes, group_table = mode_tables()
    blocks = NAZ_EL // EA

    def one_block(totals, block_id):
        start = (block_id * EA).astype(jnp.int32)

        def cut(array, axis_pos):
            return lax.dynamic_slice_in_dim(array, start, EA, axis_pos)

        faces = jnp.stack([cut(trace_azimuth, 1), cut(behind_azimuth, 1), cut(trace_radial, 1), cut(behind_radial, 1)]).reshape(4 * FACE, -1)
        flags = cut(order, 0).reshape(-1) == 5
        keep = lower_modes[:, None] | flags[None, :]
        adjoint = jnp.where(keep, jnp.dot(lift_map, faces, preferred_element_type=jnp.float32), 0.0)
        values = jnp.where(keep, cut(state, 1).reshape(KMAX, -1), jnp.zeros((), jnp.bfloat16))
        residual = jnp.where(keep, jnp.dot(jacobian, values, preferred_element_type=jnp.float32), 0.0)
        contrib = jnp.dot(group_table, adjoint * residual, precision=lax.Precision.HIGHEST, preferred_element_type=jnp.float32)
        owners = cut(patch, 0).reshape(-1)
        return totals + jax.ops.segment_sum(contrib.T, owners, num_segments=NP), None

    totals, unused = lax.scan(one_block, jnp.zeros((NP, GROUPS), jnp.float32), jnp.arange(blocks, dtype=jnp.int32))
    return jnp.abs(totals)
```

```python
import functools

import jax
import jax.numpy as jnp
from jax import lax
from jax.experimental import pallas as pl
from jax.experimental.pallas import tpu as pltpu
from jax.sharding import PartitionSpec as P

DEG = 6
MODES = DEG**3
VARS = 5
DIRS = 3
GROUPS = VARS * DIRS * DEG
PER_VAR = DIRS * DEG
GROUP_ROWS = 24
PATCH_DEV = 48
BAND = 16
ROWS = 8
LANES = 128
SLOTS = 64
SEATS = 2
VLIM = 57 * 1024 * 1024
PARTS = (((0, 1), (2,)), ((3, 4),))
MESH_ID = pl.DeviceIdType.MESH


def iota(shape, dim):
    return lax.broadcasted_iota(jnp.int32, shape, dim)


def stacked_halves(value):
    high = value.astype(jnp.bfloat16).astype(jnp.float32)
    return high, value - high


def table_dot(value, table):
    rows = value.shape[0]
    both = jnp.concatenate(stacked_halves(value), axis=0).astype(jnp.bfloat16)
    sums = jnp.dot(both, table, preferred_element_type=jnp.float32)
    return sums[:rows] + sums[rows:]


def group_table():
    group = iota((GROUP_ROWS, MODES), 0)
    mode = iota((GROUP_ROWS, MODES), 1)
    direction, degree = group // DEG, group % DEG
    of_mode = jnp.where(direction == 0, mode // (DEG * DEG), jnp.where(direction == 1, mode // DEG % DEG, mode % DEG))
    hit = (of_mode == degree) & (group < PER_VAR)
    return hit.astype(jnp.float32).astype(jnp.bfloat16)


def lower_modes():
    mode = iota((MODES, LANES), 0)
    most = jnp.maximum(jnp.maximum(mode // (DEG * DEG), mode // DEG % DEG), mode % DEG)
    return (most <= DEG - 2).astype(jnp.float32)


def fused_kernel(
    n_z, n_seat, n_rad, ta_hbm, tr_hbm, st_hbm, jac_hbm, lift_hbm, order_hbm, patch_hbm, out_ref,
    ta, tr, st, jac, lift_t, lift, order, patch, values, faces, acc, flat_r,
    rim_out, rim_in, ids_out, ids_in, choose, rows_out, rows_in, sums_out, sums_in,
    load_sem, state_sem, rim_sem, ids_sem, gather_sem, sum_sem,
):
    azi, rad = lax.axis_index("azi"), lax.axis_index("rad")
    n_azi = n_z * n_seat
    z, seat = azi // n_seat, azi % n_seat
    targets = n_seat * n_rad
    me = seat * n_rad + rad
    face_len, rows_azi, _ = ta.shape
    kmax = jac.shape[0]
    blocks = rows_azi // ROWS
    bands = rows_azi // BAND
    width = ROWS * LANES
    pairs = sum(len(part) for part in PARTS)

    def towards(by_azi, by_rad):
        return {"azi": (azi + n_azi + by_azi) % n_azi, "rad": (rad + n_rad + by_rad) % n_rad}

    def at_z(peer):
        return {"azi": peer * n_seat + seat, "rad": rad}

    def at_target(peer):
        return {"azi": z * n_seat + peer // n_rad, "rad": peer % n_rad}

    barrier = pltpu.get_barrier_semaphore()
    senders = [towards(-1, 0), towards(0, -1)]
    senders += [at_z((z + k) % n_z) for k in range(1, n_z)]
    senders += [at_target((me + k) % targets) for k in range(1, targets)]
    for device in senders:
        pl.semaphore_signal(barrier, inc=1, device_id=device, device_id_type=MESH_ID)

    spans = []
    first_var = 0
    for part in PARTS:
        count = sum(len(pair) for pair in part)
        spans.append((first_var * MODES, count * MODES))
        first_var += count

    loads = [
        pltpu.make_async_copy(order_hbm, order, load_sem.at[0]),
        pltpu.make_async_copy(patch_hbm, patch, load_sem.at[1]),
        pltpu.make_async_copy(tr_hbm, tr, load_sem.at[2]),
        pltpu.make_async_copy(ta_hbm, ta, load_sem.at[3]),
        pltpu.make_async_copy(lift_hbm, lift_t, load_sem.at[4]),
    ]
    jac_loads = [
        pltpu.make_async_copy(jac_hbm.at[pl.ds(start, count)], jac.at[pl.ds(start, count)], load_sem.at[5 + i])
        for i, (start, count) in enumerate(spans)
    ]
    state_loads = [
        pltpu.make_async_copy(st_hbm.at[:, pl.ds(b * ROWS, ROWS), :], st.at[b], state_sem.at[b])
        for b in range(blocks)
    ]
    for copy in loads + [state_loads[0], jac_loads[0]] + state_loads[1:] + jac_loads[1:]:
        copy.start()

    loads[2].wait()
    flat_r[...] = tr[...].reshape(face_len, rows_azi * LANES)
    lane = iota((face_len, LANES), 1)
    column = jnp.zeros((face_len, LANES), jnp.float32)
    for i in range(rows_azi):
        piece = flat_r[:, i * LANES : (i + 1) * LANES].astype(jnp.float32)
        column = jnp.where(lane == i, pltpu.roll(piece, (i + 1) % LANES, 1), column)
    rim_out[1] = column.astype(jnp.bfloat16)
    loads[3].wait()
    rim_out[0] = ta[:, rows_azi - 1, :]

    loads[0].wait()
    loads[1].wait()
    upto = (iota((LANES, LANES), 0) <= iota((LANES, LANES), 1)).astype(jnp.float32).astype(jnp.bfloat16)
    since = iota((LANES, LANES), 1) <= iota((LANES, LANES), 0)
    ones = jnp.ones((LANES, LANES), jnp.bfloat16)
    used = jnp.zeros((1, LANES), jnp.float32)
    ids = jnp.zeros((SLOTS, 1), jnp.float32)
    slot = iota((SLOTS, LANES), 0).astype(jnp.float32)
    slot_of = []
    for band in range(bands):
        row = patch[band * BAND : band * BAND + ROWS].astype(jnp.float32)
        start = jnp.where((iota(row.shape, 1) == 0) | (row != pltpu.roll(row, 1, 1)), 1.0, 0.0)
        rank_row = jnp.dot(start.astype(jnp.bfloat16), upto, preferred_element_type=jnp.float32)[:1] - 1.0 + used
        begun = jnp.where(since, start[:1], 0.0).astype(jnp.bfloat16)
        rank_col = jnp.dot(begun, ones, preferred_element_type=jnp.float32)
        mine = (slot == rank_row) & (start[:1] > 0.0)
        ids = ids + jnp.sum(jnp.where(mine, row[:1] + 1.0, 0.0), axis=1, keepdims=True)
        slot_of.append(rank_col - 1.0 + used)
        used = used + rank_col[LANES - 1 :]
    ids_out[...] = jnp.broadcast_to(ids - 1.0, ids_out.shape)
    ids_in[z] = ids_out[...]

    def rim_copy(which, target):
        return pltpu.make_async_remote_copy(
            src_ref=rim_out.at[which], dst_ref=rim_in.at[which],
            send_sem=rim_sem.at[0, which], recv_sem=rim_sem.at[1, which],
            device_id=target, device_id_type=MESH_ID,
        )

    def ids_copy(peer, source):
        return pltpu.make_async_remote_copy(
            src_ref=ids_out, dst_ref=ids_in.at[source],
            send_sem=ids_sem.at[0, peer], recv_sem=ids_sem.at[1, source],
            device_id=at_z(peer), device_id_type=MESH_ID,
        )

    def gather_copy(part, peer, source):
        span = pl.ds(pair_start[part], len(PARTS[part]))
        return pltpu.make_async_remote_copy(
            src_ref=rows_out.at[span], dst_ref=rows_in.at[source, span],
            send_sem=gather_sem.at[0, part, peer], recv_sem=gather_sem.at[1, part, source],
            device_id=at_z(peer), device_id_type=MESH_ID,
        )

    def sum_copy(part, peer, source):
        span = pl.ds(pair_start[part], len(PARTS[part]))
        return pltpu.make_async_remote_copy(
            src_ref=sums_out.at[peer, span], dst_ref=sums_in.at[source, span],
            send_sem=sum_sem.at[0, part, peer], recv_sem=sum_sem.at[1, part, source],
            device_id=at_target(peer), device_id_type=MESH_ID,
        )

    pair_start = [sum(len(part) for part in PARTS[:i]) for i in range(len(PARTS))]
    z_peers = [((z + k) % n_z, (z + n_z - k) % n_z) for k in range(1, n_z)]
    plane_peers = [((me + k) % targets, (me + targets - k) % targets) for k in range(1, targets)]

    pl.semaphore_wait(barrier, len(senders))
    rims = [rim_copy(0, towards(1, 0)), rim_copy(1, towards(0, 1))]
    for copy in rims:
        copy.start()
    for peer, source in z_peers:
        ids_copy(peer, z).start()

    loads[4].wait()
    lift[...] = lift_t[...].T
    lower = lower_modes()
    table = group_table()
    lower_all = jnp.concatenate([lower] * VARS, axis=0)
    lower_all_16 = lower_all.astype(jnp.bfloat16)

    def flag_row(row):
        return (order[row : row + 1] == DEG - 1).astype(jnp.float32)

    def stage_values(b):
        keep = jnp.concatenate(
            [jnp.maximum(lower_all, flag_row(b * ROWS + i)).astype(jnp.bfloat16) for i in range(ROWS)], axis=1
        )
        values[b] = st[b].reshape(kmax, width) * keep

    def stage_faces(b):
        ta_b = ta[:, b * ROWS : (b + 1) * ROWS, :].reshape(face_len, width)
        if b == 0:
            before = rim_in[0]
        else:
            before = ta[:, b * ROWS - 1, :]
        tr_b = flat_r[:, b * width : (b + 1) * width]
        rim = rim_in[1].astype(jnp.float32)
        pieces = []
        for i in range(ROWS):
            moved = pltpu.roll(tr_b[:, i * LANES : (i + 1) * LANES].astype(jnp.float32), 1, 1)
            row = b * ROWS + i
            edge = pltpu.roll(rim, (LANES - row) % LANES, 1)
            pieces.append(jnp.where(lane == 0, jnp.where(rad > 0, edge, 0.0), moved).astype(jnp.bfloat16))
        faces[b, 0:face_len] = ta_b
        faces[b, face_len : 2 * face_len] = jnp.concatenate([before, ta_b[:, : width - LANES]], axis=1)
        faces[b, 2 * face_len : 3 * face_len] = tr_b
        faces[b, 3 * face_len :] = jnp.concatenate(pieces, axis=1)

    def weigh(part, b, residual):
        start, count = spans[part]
        adjoint = jnp.dot(lift[start : start + count], faces[b], preferred_element_type=jnp.float32)
        low = lower_all[start : start + count]
        total = None
        for i in range(ROWS):
            cut = slice(i * LANES, (i + 1) * LANES)
            term = adjoint[:, cut] * residual[:, cut] * jnp.maximum(low, flag_row(b * ROWS + i))
            total = term if total is None else total + term
        return total

    def residual_of(part, b):
        start, count = spans[part]
        return jnp.dot(jac[start : start + count], values[b], preferred_element_type=jnp.float32)

    def add_block(part, b, total):
        start, count = spans[part]
        band = b * ROWS // BAND
        if b * ROWS % BAND == 0:
            acc[band, start : start + count] = total
        else:
            acc[band, start : start + count] += total

    def grouped(var, band):
        both = stacked_halves(acc[band, var * MODES : (var + 1) * MODES])
        both = jnp.concatenate(both, axis=1).astype(jnp.bfloat16)
        sums = jnp.dot(table, both, preferred_element_type=jnp.float32)
        return sums[:, :LANES] + sums[:, LANES:]

    slot_lane = iota((LANES, LANES), 1).astype(jnp.float32)

    def send_rows(part):
        for p, pair in enumerate(PARTS[part], pair_start[part]):
            terms = []
            tables = []
            for side, var in enumerate(pair):
                for band in range(bands):
                    terms.append(grouped(var, band))
                    hit = slot_of[band] == slot_lane - float(side * SLOTS)
                    tables.append(hit.astype(jnp.float32).astype(jnp.bfloat16))
            rows_out[p] = table_dot(jnp.concatenate(terms, axis=1), jnp.concatenate(tables, axis=0))
        for peer, source in z_peers:
            gather_copy(part, peer, z).start()
        span = pl.ds(pair_start[part], len(PARTS[part]))
        rows_in[z, span] = rows_out[span]

    def send_sums(part):
        for peer, source in z_peers:
            gather_copy(part, peer, source).wait_recv()
        for p in range(pair_start[part], pair_start[part] + len(PARTS[part])):
            terms = jnp.concatenate([rows_in[peer, p] for peer in range(n_z)], axis=1)
            sums = table_dot(terms, choose[...])
            for target in range(targets):
                sums_out[target, p] = sums[:, target * LANES : (target + 1) * LANES]
        for peer, source in plane_peers:
            sum_copy(part, peer, me).start()
        span = pl.ds(pair_start[part], len(PARTS[part]))
        sums_in[me, span] = sums_out[me, span]

    def make_choose():
        for peer, source in z_peers:
            ids_copy(peer, source).wait_recv()
        here = iota((1, LANES), 1)
        sides = []
        for side in range(2):
            inside = (here >= side * PATCH_DEV) & (here < (side + 1) * PATCH_DEV)
            sides.append(jnp.where(inside, here - side * PATCH_DEV, -(2**20)).astype(jnp.float32))
        base = (z * targets * PATCH_DEV).astype(jnp.float32)
        for peer in range(n_z):
            for side in range(2):
                begin = (2 * peer + side) * SLOTS
                for target in range(targets):
                    hit = ids_in[peer] == sides[side] + (base + float(target * PATCH_DEV))
                    choose[begin : begin + SLOTS, target * LANES : (target + 1) * LANES] = hit.astype(
                        jnp.float32
                    ).astype(jnp.bfloat16)

    state_loads[0].wait()
    stage_values(0)
    jac_loads[0].wait()
    first = residual_of(0, 0)
    for copy in rims:
        copy.wait_recv()
    stage_faces(0)
    add_block(0, 0, weigh(0, 0, first))
    for b in range(1, blocks):
        state_loads[b].wait()
        stage_values(b)
        stage_faces(b)
        add_block(0, b, weigh(0, b, residual_of(0, b)))
    send_rows(0)
    jac_loads[1].wait()
    for b in range(blocks):
        add_block(1, b, weigh(1, b, residual_of(1, b)))
        if b == 0:
            make_choose()
        if b == min(1, blocks - 1):
            send_sums(0)
    send_rows(1)
    send_sums(1)
    for part in range(len(PARTS)):
        for peer, source in plane_peers:
            sum_copy(part, peer, source).wait_recv()
    total = functools.reduce(jnp.add, [sums_in[source] for source in range(targets)])
    total = jnp.abs(total).reshape(pairs * GROUP_ROWS, LANES)
    pad = jnp.zeros((LANES - pairs * GROUP_ROWS, LANES), jnp.float32)
    turned = jnp.concatenate([total, pad], axis=0).T
    columns = []
    p = 0
    for part in PARTS:
        for pair in part:
            for side in range(len(pair)):
                columns.append(
                    turned[side * PATCH_DEV : (side + 1) * PATCH_DEV, p * GROUP_ROWS : p * GROUP_ROWS + PER_VAR]
                )
            p += 1
    out_ref[...] = jnp.concatenate(columns, axis=1)

    for copy in rims:
        copy.wait_send()
    for peer, source in z_peers:
        ids_copy(peer, z).wait_send()
    for part in range(len(PARTS)):
        for peer, source in z_peers:
            gather_copy(part, peer, z).wait_send()
        for peer, source in plane_peers:
            sum_copy(part, peer, me).wait_send()


def per_device(trace_azimuth, trace_radial, state, jacobian, lift_map, order, patch):
    face_len, rows_azi, rows_rad = trace_azimuth.shape
    kmax = jacobian.shape[0]
    n_azi, n_rad = lax.axis_size("azi"), lax.axis_size("rad")
    n_seat = SEATS if n_azi % SEATS == 0 else 1
    n_z, targets = n_azi // n_seat, n_seat * n_rad
    blocks = rows_azi // ROWS
    width = ROWS * LANES
    pairs = sum(len(part) for part in PARTS)
    f32, b16 = jnp.float32, jnp.bfloat16
    return pl.pallas_call(
        functools.partial(fused_kernel, n_z, n_seat, n_rad),
        out_shape=jax.ShapeDtypeStruct((PATCH_DEV, GROUPS), f32),
        in_specs=[pl.BlockSpec(memory_space=pl.ANY)] * 7,
        out_specs=pl.BlockSpec(memory_space=pltpu.VMEM),
        scratch_shapes=[
            pltpu.VMEM(trace_azimuth.shape, b16),
            pltpu.VMEM(trace_radial.shape, b16),
            pltpu.VMEM((blocks, kmax, ROWS, LANES), b16),
            pltpu.VMEM(jacobian.shape, b16),
            pltpu.VMEM(lift_map.shape[::-1], b16),
            pltpu.VMEM(lift_map.shape, b16),
            pltpu.VMEM(order.shape, jnp.int32),
            pltpu.VMEM(patch.shape, jnp.int32),
            pltpu.VMEM((blocks, kmax, width), b16),
            pltpu.VMEM((blocks, 4 * face_len, width), b16),
            pltpu.VMEM((rows_azi // BAND, kmax, LANES), f32),
            pltpu.VMEM((face_len, rows_azi * LANES), b16),
            pltpu.VMEM((2, face_len, LANES), b16),
            pltpu.VMEM((2, face_len, LANES), b16),
            pltpu.VMEM((SLOTS, LANES), f32),
            pltpu.VMEM((n_z, SLOTS, LANES), f32),
            pltpu.VMEM((n_z * 2 * SLOTS, targets * LANES), b16),
            pltpu.VMEM((pairs, GROUP_ROWS, LANES), f32),
            pltpu.VMEM((n_z, pairs, GROUP_ROWS, LANES), f32),
            pltpu.VMEM((targets, pairs, GROUP_ROWS, LANES), f32),
            pltpu.VMEM((targets, pairs, GROUP_ROWS, LANES), f32),
            pltpu.SemaphoreType.DMA((5 + len(PARTS),)),
            pltpu.SemaphoreType.DMA((blocks,)),
            pltpu.SemaphoreType.DMA((2, 2)),
            pltpu.SemaphoreType.DMA((2, n_z)),
            pltpu.SemaphoreType.DMA((2, len(PARTS), n_z)),
            pltpu.SemaphoreType.DMA((2, len(PARTS), targets)),
        ],
        compiler_params=pltpu.CompilerParams(collective_id=0, has_side_effects=True, vmem_limit_bytes=VLIM),
        cost_estimate=pl.CostEstimate(
            flops=2 * kmax * (kmax + 4 * face_len) * rows_azi * rows_rad,
            bytes_accessed=2 * kmax * rows_azi * rows_rad, transcendentals=0,
        ),
    )(trace_azimuth, trace_radial, state, jacobian, lift_map.T, order, patch)


def solution(mesh):
    in_specs = (
        P(None, "azi", "rad"),
        P(None, "azi", "rad"),
        P(None, "azi", "rad"),
        P(),
        P(),
        P("azi", "rad"),
        P("azi", "rad"),
    )
    out_specs = P(("azi", "rad"), None)
    return jax.shard_map(
        per_device, mesh=mesh, in_specs=in_specs, out_specs=out_specs, check_vma=False
    )
```

```python
import functools

import jax
import jax.numpy as jnp
import numpy as np
from jax import lax
from jax.experimental import pallas as pl
from jax.experimental.pallas import tpu as pltpu
from jax.sharding import PartitionSpec as P

DEG = 6
MODES = 216
KMAX = 1080
GROUPS = 90
PATCH_DEV = 48
BAND = 16
ROWS = 8
LANES = 128
SLOTS = 56
ID_LANE = LANES - 1
SUBS = 1
VLIM_RIM = 57 * 1024 * 1024
VLIM_MAIN = 57 * 1024 * 1024
SEATS = 2
DIRS = 3
VARS = 5
PER_VAR = DIRS * DEG
GROUP_ROWS = 24
RUN_SLOTS = 64
FLAG_SLOT = RUN_SLOTS - 1
DEPTH = 256
VLIM = 57 * 1024 * 1024
PARTS = (((0, 1), (2,)), ((3, 4),))
MESH_ID = pl.DeviceIdType.MESH


def rim_kernel(n_azi, n_rad, ta_ref, tr_ref, rim_a_ref, rim_r_ref, outgoing, recv, send_sem, recv_sem):
    azi, rad = lax.axis_index("azi"), lax.axis_index("rad")
    mesh_id = pl.DeviceIdType.MESH
    barrier = pltpu.get_barrier_semaphore()

    def towards(by_azi, by_rad):
        return {"azi": (azi + n_azi + by_azi) % n_azi, "rad": (rad + n_rad + by_rad) % n_rad}

    pl.semaphore_signal(barrier, inc=1, device_id=towards(-1, 0), device_id_type=mesh_id)
    pl.semaphore_signal(barrier, inc=1, device_id=towards(0, -1), device_id_type=mesh_id)

    outgoing[0] = ta_ref[:, ta_ref.shape[1] - 1, :]
    face_len, rows_azi, lanes = tr_ref.shape
    flat = tr_ref[...].reshape(face_len, rows_azi * lanes)
    lane = lax.broadcasted_iota(jnp.int32, (face_len, lanes), 1)
    column = jnp.zeros((face_len, lanes), jnp.float32)
    for i in range(rows_azi):
        piece = flat[:, i * lanes : (i + 1) * lanes].astype(jnp.float32)
        column = jnp.where(lane == i, pltpu.roll(piece, (i + 1) % lanes, 1), column)
    outgoing[1] = column.astype(jnp.bfloat16)

    pl.semaphore_wait(barrier, 2)
    copies = []
    for slot, target in enumerate((towards(1, 0), towards(0, 1))):
        copies.append(
            pltpu.make_async_remote_copy(
                src_ref=outgoing.at[slot], dst_ref=recv.at[slot],
                send_sem=send_sem.at[slot], recv_sem=recv_sem.at[slot],
                device_id=target, device_id_type=mesh_id,
            )
        )
    for copy in copies:
        copy.start()
    for copy in copies:
        copy.wait()
    rim_a_ref[...] = recv[0]
    rim_r_ref[...] = jnp.where(rad > 0, recv[1], jnp.zeros_like(recv[1]))


def mode_tables():
    mode_index = np.arange(KMAX)
    variable = mode_index // MODES
    inside = mode_index % MODES
    degrees = [inside // (DEG * DEG), inside // DEG % DEG, inside % DEG]
    lower_modes = np.maximum(np.maximum(degrees[0], degrees[1]), degrees[2]) <= DEG - 2
    group_index = np.arange(LANES)
    group_table = np.zeros((LANES, KMAX), np.float32)
    for direction in range(3):
        target = variable * 3 * DEG + direction * DEG + degrees[direction]
        group_table = group_table + (group_index[:, None] == target[None, :]).astype(np.float32)
    return (lower_modes, group_table)


def halves(value):
    high = value.astype(jnp.bfloat16)
    low = (value - high.astype(jnp.float32)).astype(jnp.bfloat16)
    return high, low


def exact_table_dot(table, value):
    high, low = halves(value)
    dims = (((1,), (1,)), ((), ()))
    return lax.dot_general(table, high, dims, preferred_element_type=jnp.float32) + lax.dot_general(
        table, low, dims, preferred_element_type=jnp.float32
    )


def slot_ids_of_runs(patch, rows_azi):
    slot = lax.broadcasted_iota(jnp.int32, (SLOTS, LANES), 0).astype(jnp.float32)
    upto = lax.broadcasted_iota(jnp.int32, (LANES, LANES), 0) <= lax.broadcasted_iota(
        jnp.int32, (LANES, LANES), 1
    )
    used = jnp.zeros((1, 1), jnp.float32)
    ids = jnp.zeros((SLOTS, 1), jnp.float32)
    for band in range(0, rows_azi, BAND):
        row = patch[band : band + 8].astype(jnp.float32)
        lane = lax.broadcasted_iota(jnp.int32, row.shape, 1)
        start = jnp.where((lane == 0) | (row != pltpu.roll(row, 1, 1)), 1.0, 0.0)
        rank = jnp.dot(
            start.astype(jnp.bfloat16), upto.astype(jnp.bfloat16), preferred_element_type=jnp.float32
        )
        mine = (slot == rank[:1] - 1.0 + used) & (start[:1] > 0.0)
        ids = ids + jnp.sum(jnp.where(mine, row[:1] + 1.0, 0.0), axis=1, keepdims=True)
        used = used + jnp.sum(start[:1], axis=1, keepdims=True)
    return ids.astype(jnp.int32) - 1


def local_kernel(
    ta_ref, tr_ref, st_ref, jac_ref, lift_ref, order_ref, patch_ref, lower_ref, table_ref,
    rim_a_ref, rim_r_ref, out_ref, carry, acc, lift, slots, jac, jac_sem,
):
    step = pl.program_id(0)
    fetch = pltpu.make_async_copy(jac_ref, jac, jac_sem)

    @pl.when(step == 0)
    def _():
        fetch.start()

    width = ROWS * LANES
    rows_azi = patch_ref.shape[0]
    face_len = ta_ref.shape[0]
    steps_band = BAND // ROWS

    all_patch = patch_ref[...]
    differ = jnp.int32(0)
    for band in range(0, rows_azi, BAND):
        rows = all_patch[band : band + BAND]
        differ = jnp.maximum(differ, jnp.max((rows != rows[:1]).astype(jnp.int32)))

    @pl.when(step == 0)
    def _():
        carry[...] = rim_a_ref[...]
        out_ref[...] = jnp.zeros_like(out_ref)
        lift[...] = lift_ref[...].T
        slots[...] = jnp.broadcast_to(slot_ids_of_runs(all_patch, rows_azi), slots.shape)

    @pl.when((step == 0) & (differ != 0))
    def _():
        none = jnp.int32(2**30)
        where_slot = lax.broadcasted_iota(jnp.int32, slots.shape, 0)

        def next_id(slot, last):
            found = jnp.min(jnp.where(all_patch > last, all_patch, none))
            slots[...] = jnp.where(where_slot == slot, jnp.where(found == none, -1, found), slots[...])
            return found

        lax.fori_loop(0, SLOTS, next_id, jnp.int32(-1))

    ta = ta_ref[...].reshape(face_len, width)
    tr = tr_ref[...].reshape(face_len, width)
    behind_a = jnp.concatenate([carry[...], ta[:, : width - LANES]], axis=1)
    carry[...] = ta[:, width - LANES :]
    row_id = lax.broadcasted_iota(jnp.int32, (rows_azi, width), 0)
    lane_id = lax.broadcasted_iota(jnp.int32, (rows_azi, width), 1)
    spread = ((row_id - step * ROWS) * LANES == lane_id).astype(jnp.bfloat16)
    rim = jnp.dot(rim_r_ref[:, :rows_azi], spread, preferred_element_type=jnp.float32)
    moved = pltpu.roll(tr.astype(jnp.float32), 1, 1)
    first = lax.broadcasted_iota(jnp.int32, (face_len, width), 1) % LANES == 0
    behind_r = jnp.where(first, rim, moved).astype(jnp.bfloat16)
    faces = jnp.concatenate([ta, behind_a, tr, behind_r], axis=0)

    @pl.when(step == 0)
    def _():
        fetch.wait()

    flags = (order_ref[...] == DEG - 1).astype(jnp.float32)
    sub = ROWS // SUBS

    def product_rows(index):
        span = slice(index * sub, (index + 1) * sub)
        cut = slice(index * sub * LANES, (index + 1) * sub * LANES)
        keep = jnp.maximum(lower_ref[...], flags[span].reshape(1, sub * LANES))
        values = st_ref[:, span, :].reshape(KMAX, sub * LANES) * keep.astype(jnp.bfloat16)
        adjoint = jnp.dot(lift[...], faces[:, cut], preferred_element_type=jnp.float32)
        residual = jnp.dot(jac[...], values, preferred_element_type=jnp.float32)
        product = adjoint * residual * keep
        return [product[:, row * LANES : (row + 1) * LANES] for row in range(sub)]

    band_start = pl.multiple_of(step // steps_band * BAND, BAND)
    band_row = patch_ref[pl.ds(band_start, 1), :]
    mine = patch_ref[pl.ds(pl.multiple_of(step * ROWS, ROWS), ROWS), :]
    place = slots[...]

    def add_to_patches(columns, row):
        grouped = exact_grouped(columns)
        chosen = (place == row).astype(jnp.bfloat16)
        out_ref[...] += exact_table_dot(chosen, grouped)

    def exact_grouped(columns):
        both = jnp.concatenate(halves(columns), axis=1)
        sums = jnp.dot(table_ref[...], both, preferred_element_type=jnp.float32)
        return sums[:, :LANES] + sums[:, LANES:]

    @pl.when(step % steps_band == 0)
    def _():
        acc[...] = jnp.zeros_like(acc)

    @pl.when(differ == 0)
    def _():
        for index in range(SUBS):
            acc[...] += functools.reduce(jnp.add, product_rows(index))

    @pl.when(differ != 0)
    def _():
        for index in range(SUBS):
            for row, product in enumerate(product_rows(index), index * sub):
                add_to_patches(product, mine[row : row + 1])

    @pl.when(step % steps_band == steps_band - 1)
    def _():
        @pl.when(differ == 0)
        def _():
            add_to_patches(acc[...], band_row)

    @pl.when(step == pl.num_programs(0) - 1)
    def _():
        lane = lax.broadcasted_iota(jnp.int32, out_ref.shape, 1)
        out_ref[...] = jnp.where(lane == ID_LANE, place.astype(jnp.float32), out_ref[...])


def exchange_kernel(
    n_z, n_seat, n_rad, rows_ref, out_ref, gathered, outgoing, recv,
    gather_send, gather_recv, sum_send, sum_recv,
):
    azi, rad = lax.axis_index("azi"), lax.axis_index("rad")
    z, seat = azi // n_seat, azi % n_seat
    targets = n_seat * n_rad
    me = seat * n_rad + rad
    mesh_id = pl.DeviceIdType.MESH

    def at_z(peer):
        return {"azi": peer * n_seat + seat, "rad": rad}

    def at_target(peer):
        return {"azi": z * n_seat + peer // n_rad, "rad": peer % n_rad}

    barrier = pltpu.get_barrier_semaphore()
    for k in range(1, n_z):
        pl.semaphore_signal(barrier, inc=1, device_id=at_z((z + k) % n_z), device_id_type=mesh_id)
    for k in range(1, targets):
        pl.semaphore_signal(
            barrier, inc=1, device_id=at_target((me + k) % targets), device_id_type=mesh_id
        )
    pl.semaphore_wait(barrier, n_z + targets - 2)

    def gather_copy(peer, source):
        return pltpu.make_async_remote_copy(
            src_ref=rows_ref, dst_ref=gathered.at[source],
            send_sem=gather_send.at[peer], recv_sem=gather_recv.at[source],
            device_id=at_z(peer), device_id_type=mesh_id,
        )

    def sum_copy(peer, source):
        return pltpu.make_async_remote_copy(
            src_ref=outgoing.at[peer], dst_ref=recv.at[source],
            send_sem=sum_send.at[peer], recv_sem=sum_recv.at[source],
            device_id=at_target(peer), device_id_type=mesh_id,
        )

    for k in range(1, n_z):
        gather_copy((z + k) % n_z, z).start()
    gathered[z] = rows_ref[...]
    for k in range(1, n_z):
        gather_copy((z + k) % n_z, (z + n_z - k) % n_z).wait_recv()

    rows = gathered[...].reshape(n_z * SLOTS, LANES)
    pick = (lax.broadcasted_iota(jnp.int32, (8, LANES), 1) == ID_LANE).astype(jnp.bfloat16)
    ids = exact_table_dot(pick, rows)[:1]
    count = targets * PATCH_DEV
    wanted = (z * count + lax.broadcasted_iota(jnp.int32, (count, n_z * SLOTS), 0)).astype(jnp.float32)
    chosen = (wanted == ids).astype(jnp.bfloat16)
    both = jnp.dot(
        chosen, jnp.concatenate(halves(rows), axis=1), preferred_element_type=jnp.float32
    )
    outgoing[...] = (both[:, :LANES] + both[:, LANES:]).reshape(targets, PATCH_DEV, LANES)

    for k in range(1, targets):
        sum_copy((me + k) % targets, me).start()
    total = outgoing[me]
    for k in range(1, targets):
        source = (me + targets - k) % targets
        sum_copy((me + k) % targets, source).wait_recv()
        total = total + recv[source]
    for k in range(1, n_z):
        gather_copy((z + k) % n_z, z).wait_send()
    for k in range(1, targets):
        sum_copy((me + k) % targets, me).wait_send()
    out_ref[...] = jnp.abs(total)[:, : out_ref.shape[1]]


def general_path(trace_azimuth, trace_radial, state, jacobian, lift_map, order, patch):
    face_len, rows_azi, rows_rad = trace_azimuth.shape
    n_azi, n_rad = lax.axis_size("azi"), lax.axis_size("rad")
    n_seat = SEATS if n_azi % SEATS == 0 else 1
    n_z, targets = n_azi // n_seat, n_seat * n_rad
    rim = jax.ShapeDtypeStruct((face_len, LANES), jnp.bfloat16)
    rim_azimuth, rim_radial = pl.pallas_call(
        functools.partial(rim_kernel, n_azi, n_rad),
        grid=(1,),
        out_shape=(rim, rim),
        in_specs=[
            pl.BlockSpec((face_len, ROWS, LANES), lambda t: (0, rows_azi // ROWS - 1, 0)),
            pl.BlockSpec(trace_radial.shape, lambda t: (0, 0, 0)),
        ],
        out_specs=(pl.BlockSpec(rim.shape, lambda t: (0, 0)),) * 2,
        scratch_shapes=[
            pltpu.VMEM((2,) + rim.shape, jnp.bfloat16),
            pltpu.VMEM((2,) + rim.shape, jnp.bfloat16),
            pltpu.SemaphoreType.DMA((2,)),
            pltpu.SemaphoreType.DMA((2,)),
        ],
        compiler_params=pltpu.CompilerParams(
            collective_id=2, has_side_effects=True, vmem_limit_bytes=VLIM_RIM
        ),
        cost_estimate=pl.CostEstimate(flops=0, bytes_accessed=12_000_000, transcendentals=0),
    )(trace_azimuth, trace_radial)
    lower_np, group_np = mode_tables()
    lower = jnp.asarray(lower_np.astype(np.float32)[:, None])
    table = jnp.asarray(group_np, jnp.bfloat16)

    def whole(shape):
        return pl.BlockSpec(shape, lambda t: (0,) * len(shape))

    def part(depth):
        return pl.BlockSpec((depth, ROWS, LANES), lambda t: (0, t, 0))

    rows = pl.pallas_call(
        local_kernel,
        grid=(rows_azi // ROWS,),
        out_shape=jax.ShapeDtypeStruct((SLOTS, LANES), jnp.float32),
        in_specs=[
            part(face_len), part(face_len), part(KMAX),
            pl.BlockSpec(memory_space=pl.ANY), whole(lift_map.shape[::-1]),
            pl.BlockSpec((ROWS, LANES), lambda t: (t, 0)), whole(patch.shape),
            whole(lower.shape), whole(table.shape),
            whole(rim_azimuth.shape), whole(rim_radial.shape),
        ],
        out_specs=whole((SLOTS, LANES)),
        scratch_shapes=[
            pltpu.VMEM((face_len, LANES), jnp.bfloat16),
            pltpu.VMEM((KMAX, LANES), jnp.float32),
            pltpu.VMEM(lift_map.shape, jnp.bfloat16),
            pltpu.VMEM((SLOTS, LANES), jnp.int32),
            pltpu.VMEM(jacobian.shape, jnp.bfloat16),
            pltpu.SemaphoreType.DMA,
        ],
        compiler_params=pltpu.CompilerParams(
            dimension_semantics=("arbitrary",), vmem_limit_bytes=VLIM_MAIN
        ),
        cost_estimate=pl.CostEstimate(
            flops=2 * KMAX * (KMAX + 4 * face_len) * rows_azi * rows_rad,
            bytes_accessed=2 * KMAX * rows_azi * rows_rad, transcendentals=0,
        ),
    )(trace_azimuth, trace_radial, state, jacobian, lift_map.T, order, patch, lower, table,
      rim_azimuth, rim_radial)

    return pl.pallas_call(
        functools.partial(exchange_kernel, n_z, n_seat, n_rad),
        out_shape=jax.ShapeDtypeStruct((PATCH_DEV, GROUPS), jnp.float32),
        in_specs=[pl.BlockSpec(memory_space=pltpu.VMEM)],
        out_specs=pl.BlockSpec(memory_space=pltpu.VMEM),
        scratch_shapes=[
            pltpu.VMEM((n_z, SLOTS, LANES), jnp.float32),
            pltpu.VMEM((targets, PATCH_DEV, LANES), jnp.float32),
            pltpu.VMEM((targets, PATCH_DEV, LANES), jnp.float32),
            pltpu.SemaphoreType.DMA((n_z,)),
            pltpu.SemaphoreType.DMA((n_z,)),
            pltpu.SemaphoreType.DMA((targets,)),
            pltpu.SemaphoreType.DMA((targets,)),
        ],
        compiler_params=pltpu.CompilerParams(collective_id=1, has_side_effects=True),
    )(rows)


def iota(shape, dim):
    return lax.broadcasted_iota(jnp.int32, shape, dim)


def float_halves(value):
    high = value.astype(jnp.bfloat16).astype(jnp.float32)
    return high, value - high


def table_dot(value, table):
    rows = value.shape[0]
    both = jnp.concatenate(float_halves(value), axis=0).astype(jnp.bfloat16)
    sums = jnp.dot(both, table, preferred_element_type=jnp.float32)
    return sums[:rows] + sums[rows:]


def group_table():
    group = iota((GROUP_ROWS, MODES), 0)
    mode = iota((GROUP_ROWS, MODES), 1)
    direction, degree = group // DEG, group % DEG
    of_mode = jnp.where(direction == 0, mode // (DEG * DEG), jnp.where(direction == 1, mode // DEG % DEG, mode % DEG))
    hit = (of_mode == degree) & (group < PER_VAR)
    return hit.astype(jnp.float32).astype(jnp.bfloat16)


def lower_modes():
    mode = iota((MODES, LANES), 0)
    most = jnp.maximum(jnp.maximum(mode // (DEG * DEG), mode // DEG % DEG), mode % DEG)
    return (most <= DEG - 2).astype(jnp.float32)


def fused_kernel(
    n_z, n_seat, n_rad, ta_hbm, tr_hbm, st_hbm, jac_hbm, lift_hbm, order_hbm, patch_hbm, out_ref, flag_ref,
    ta, tr, st, jac, lift_t, lift, order, patch, values, faces, acc, flat_r,
    rim_out, rim_in, ids_out, ids_in, place, choose, rows_out, rows_in, sums_out, sums_in,
    load_sem, state_sem, rim_sem, ids_sem, gather_sem, sum_sem,
):
    azi, rad = lax.axis_index("azi"), lax.axis_index("rad")
    n_azi = n_z * n_seat
    z, seat = azi // n_seat, azi % n_seat
    targets = n_seat * n_rad
    me = seat * n_rad + rad
    face_len, rows_azi, _ = ta.shape
    kmax = jac.shape[0]
    blocks = rows_azi // ROWS
    bands = rows_azi // BAND
    width = ROWS * LANES

    def towards(by_azi, by_rad):
        return {"azi": (azi + n_azi + by_azi) % n_azi, "rad": (rad + n_rad + by_rad) % n_rad}

    def at_z(peer):
        return {"azi": peer * n_seat + seat, "rad": rad}

    def at_target(peer):
        return {"azi": z * n_seat + peer // n_rad, "rad": peer % n_rad}

    barrier = pltpu.get_barrier_semaphore()
    senders = [towards(-1, 0), towards(0, -1)]
    senders += [at_z((z + k) % n_z) for k in range(1, n_z)]
    senders += [at_target((me + k) % targets) for k in range(1, targets)]
    for device in senders:
        pl.semaphore_signal(barrier, inc=1, device_id=device, device_id_type=MESH_ID)

    spans = []
    first_var = 0
    for part in PARTS:
        count = sum(len(pair) for pair in part)
        spans.append((first_var * MODES, count * MODES))
        first_var += count

    loads = [
        pltpu.make_async_copy(order_hbm, order, load_sem.at[0]),
        pltpu.make_async_copy(patch_hbm, patch, load_sem.at[1]),
        pltpu.make_async_copy(tr_hbm, tr, load_sem.at[2]),
        pltpu.make_async_copy(ta_hbm, ta, load_sem.at[3]),
        pltpu.make_async_copy(lift_hbm, lift_t, load_sem.at[4]),
    ]
    jac_loads = [
        pltpu.make_async_copy(jac_hbm.at[pl.ds(start, count)], jac.at[pl.ds(start, count)], load_sem.at[5 + i])
        for i, (start, count) in enumerate(spans)
    ]
    state_loads = [
        pltpu.make_async_copy(st_hbm.at[:, pl.ds(b * ROWS, ROWS), :], st.at[b], state_sem.at[b])
        for b in range(blocks)
    ]
    for copy in loads + [state_loads[0], jac_loads[0]] + state_loads[1:] + jac_loads[1:]:
        copy.start()

    loads[2].wait()
    flat_r[...] = tr[...].reshape(face_len, rows_azi * LANES)
    lane = iota((face_len, LANES), 1)
    column = jnp.zeros((face_len, LANES), jnp.float32)
    for i in range(rows_azi):
        piece = flat_r[:, i * LANES : (i + 1) * LANES].astype(jnp.float32)
        column = jnp.where(lane == i, pltpu.roll(piece, (i + 1) % LANES, 1), column)
    rim_out[1] = column.astype(jnp.bfloat16)
    loads[3].wait()
    rim_out[0] = ta[:, rows_azi - 1, :]

    loads[0].wait()
    loads[1].wait()
    upto = (iota((LANES, LANES), 0) <= iota((LANES, LANES), 1)).astype(jnp.float32).astype(jnp.bfloat16)
    since = iota((LANES, LANES), 1) <= iota((LANES, LANES), 0)
    ones = jnp.ones((LANES, LANES), jnp.bfloat16)
    used = jnp.zeros((1, LANES), jnp.float32)
    ids = jnp.zeros((RUN_SLOTS, 1), jnp.float32)
    slot = iota((RUN_SLOTS, LANES), 0).astype(jnp.float32)
    slot_of = []
    for band in range(bands):
        row = patch[band * BAND : band * BAND + ROWS].astype(jnp.float32)
        start = jnp.where((iota(row.shape, 1) == 0) | (row != pltpu.roll(row, 1, 1)), 1.0, 0.0)
        rank_row = jnp.dot(start.astype(jnp.bfloat16), upto, preferred_element_type=jnp.float32)[:1] - 1.0 + used
        begun = jnp.where(since, start[:1], 0.0).astype(jnp.bfloat16)
        rank_col = jnp.dot(begun, ones, preferred_element_type=jnp.float32)
        mine = (slot == rank_row) & (start[:1] > 0.0)
        ids = ids + jnp.sum(jnp.where(mine, row[:1] + 1.0, 0.0), axis=1, keepdims=True)
        slot_of.append(rank_col - 1.0 + used)
        used = used + rank_col[LANES - 1 :]
    differ = jnp.zeros((1, 1), jnp.float32)
    for band in range(bands):
        rows = patch[band * BAND : (band + 1) * BAND]
        uneven = jnp.max((rows != rows[:1]).astype(jnp.float32), axis=0, keepdims=True)
        differ = jnp.maximum(differ, jnp.max(uneven, axis=1, keepdims=True))
    slot_id = jnp.broadcast_to(ids - 1.0, ids_out.shape)
    ids_out[...] = jnp.where(slot == float(FLAG_SLOT), -1.0 - differ, slot_id)
    ids_in[z] = ids_out[...]

    slot_lane = iota((LANES, LANES), 1).astype(jnp.float32)
    for side in range(2):
        for band in range(bands):
            begin = (side * bands + band) * LANES
            hit = slot_of[band] == slot_lane - float(side * RUN_SLOTS)
            place[begin : begin + LANES] = hit.astype(jnp.float32).astype(jnp.bfloat16)

    def rim_copy(which, target):
        return pltpu.make_async_remote_copy(
            src_ref=rim_out.at[which], dst_ref=rim_in.at[which],
            send_sem=rim_sem.at[0, which], recv_sem=rim_sem.at[1, which],
            device_id=target, device_id_type=MESH_ID,
        )

    def ids_copy(peer, source):
        return pltpu.make_async_remote_copy(
            src_ref=ids_out, dst_ref=ids_in.at[source],
            send_sem=ids_sem.at[0, peer], recv_sem=ids_sem.at[1, source],
            device_id=at_z(peer), device_id_type=MESH_ID,
        )

    def gather_copy(part, peer, source):
        span = pl.ds(pair_start[part], len(PARTS[part]))
        return pltpu.make_async_remote_copy(
            src_ref=rows_out.at[span], dst_ref=rows_in.at[source, span],
            send_sem=gather_sem.at[0, part, peer], recv_sem=gather_sem.at[1, part, source],
            device_id=at_z(peer), device_id_type=MESH_ID,
        )

    def sum_copy(part, peer, source):
        span = pl.ds(pair_start[part], len(PARTS[part]))
        return pltpu.make_async_remote_copy(
            src_ref=sums_out.at[peer, span], dst_ref=sums_in.at[source, span],
            send_sem=sum_sem.at[0, part, peer], recv_sem=sum_sem.at[1, part, source],
            device_id=at_target(peer), device_id_type=MESH_ID,
        )

    pair_start = [sum(len(part) for part in PARTS[:i]) for i in range(len(PARTS))]
    z_peers = [((z + k) % n_z, (z + n_z - k) % n_z) for k in range(1, n_z)]
    plane_peers = [((me + k) % targets, (me + targets - k) % targets) for k in range(1, targets)]

    pl.semaphore_wait(barrier, len(senders))
    rims = [rim_copy(0, towards(1, 0)), rim_copy(1, towards(0, 1))]
    for copy in rims:
        copy.start()
    for peer, source in z_peers:
        ids_copy(peer, z).start()

    loads[4].wait()
    lift[...] = lift_t[...].T
    lower = lower_modes()
    table = group_table()
    lower_all = jnp.concatenate([lower] * VARS, axis=0)
    lower_all_16 = lower_all.astype(jnp.bfloat16)

    def flag_row(row):
        return (order[row : row + 1] == DEG - 1).astype(jnp.float32)

    def stage_values(b):
        keep = jnp.concatenate(
            [jnp.maximum(lower_all_16, flag_row(b * ROWS + i).astype(jnp.bfloat16)) for i in range(ROWS)], axis=1
        )
        values[b] = st[b].reshape(kmax, width) * keep

    def stage_faces(b):
        ta_b = ta[:, b * ROWS : (b + 1) * ROWS, :].reshape(face_len, width)
        if b == 0:
            before = rim_in[0]
        else:
            before = ta[:, b * ROWS - 1, :]
        tr_b = flat_r[:, b * width : (b + 1) * width]
        rim = rim_in[1].astype(jnp.float32)
        pieces = []
        for i in range(ROWS):
            moved = pltpu.roll(tr_b[:, i * LANES : (i + 1) * LANES].astype(jnp.float32), 1, 1)
            row = b * ROWS + i
            edge = pltpu.roll(rim, (LANES - row) % LANES, 1)
            pieces.append(jnp.where(lane == 0, jnp.where(rad > 0, edge, 0.0), moved).astype(jnp.bfloat16))
        faces[b, 0:face_len] = ta_b
        faces[b, face_len : 2 * face_len] = jnp.concatenate([before, ta_b[:, : width - LANES]], axis=1)
        faces[b, 2 * face_len : 3 * face_len] = tr_b
        faces[b, 3 * face_len :] = jnp.concatenate(pieces, axis=1)

    def weigh(part, b, residual):
        start, count = spans[part]
        adjoint = jnp.dot(lift[start : start + count], faces[b], preferred_element_type=jnp.float32)
        low = lower_all[start : start + count]
        total = None
        for i in range(ROWS):
            cut = slice(i * LANES, (i + 1) * LANES)
            term = adjoint[:, cut] * residual[:, cut] * jnp.maximum(low, flag_row(b * ROWS + i))
            total = term if total is None else total + term
        return total

    def residual_of(part, b):
        start, count = spans[part]
        return jnp.dot(jac[start : start + count], values[b], preferred_element_type=jnp.float32)

    def add_block(part, b, total):
        start, count = spans[part]
        band = b * ROWS // BAND
        if b * ROWS % BAND == 0:
            acc[band, start : start + count] = total
        else:
            acc[band, start : start + count] += total

    def send_rows(part):
        halves_of = []
        for var in [var for pair in PARTS[part] for var in pair]:
            for band in range(bands):
                halves_of += float_halves(acc[band, var * MODES : (var + 1) * MODES])
        both = jnp.concatenate(halves_of, axis=1).astype(jnp.bfloat16)
        sums = jnp.dot(table, both, preferred_element_type=jnp.float32)
        begin = 0
        for p, pair in enumerate(PARTS[part], pair_start[part]):
            terms = []
            for i in range(len(pair) * bands):
                at = begin + 2 * i * LANES
                terms.append(sums[:, at : at + LANES] + sums[:, at + LANES : at + 2 * LANES])
            begin += 2 * len(terms) * LANES
            rows_out[p] = table_dot(jnp.concatenate(terms, axis=1), place[: len(terms) * LANES])
        for peer, source in z_peers:
            gather_copy(part, peer, z).start()
        span = pl.ds(pair_start[part], len(PARTS[part]))
        rows_in[z, span] = rows_out[span]

    def send_sums(part):
        for peer, source in z_peers:
            gather_copy(part, peer, source).wait_recv()
        flags = [ids_in[peer, FLAG_SLOT : FLAG_SLOT + 1] for peer in range(n_z)]
        flag = -1.0 - functools.reduce(jnp.minimum, flags)
        for p in range(pair_start[part], pair_start[part] + len(PARTS[part])):
            terms = jnp.concatenate([rows_in[peer, p] for peer in range(n_z)], axis=1)
            sums = table_dot(terms, choose[...])
            for target in range(targets):
                piece = sums[:, target * LANES : (target + 1) * LANES]
                if p == 0:
                    piece = jnp.where(iota(piece.shape, 0) == GROUP_ROWS - 1, flag, piece)
                sums_out[target, p] = piece
        for peer, source in plane_peers:
            sum_copy(part, peer, me).start()
        span = pl.ds(pair_start[part], len(PARTS[part]))
        sums_in[me, span] = sums_out[me, span]

    def make_choose():
        for peer, source in z_peers:
            ids_copy(peer, source).wait_recv()
        here = iota((1, LANES), 1)
        sides = []
        for side in range(2):
            inside = (here >= side * PATCH_DEV) & (here < (side + 1) * PATCH_DEV)
            sides.append(jnp.where(inside, here - side * PATCH_DEV, -(2**20)).astype(jnp.float32))
        base = (z * targets * PATCH_DEV).astype(jnp.float32)
        for peer in range(n_z):
            for side in range(2):
                begin = (2 * peer + side) * RUN_SLOTS
                for target in range(targets):
                    hit = ids_in[peer] == sides[side] + (base + float(target * PATCH_DEV))
                    choose[begin : begin + RUN_SLOTS, target * LANES : (target + 1) * LANES] = hit.astype(
                        jnp.float32
                    ).astype(jnp.bfloat16)

    state_loads[0].wait()
    stage_values(0)
    jac_loads[0].wait()
    first = residual_of(0, 0)
    state_loads[1].wait()
    stage_values(1)
    second = residual_of(0, 1)
    for copy in rims:
        copy.wait_recv()
    for b in range(blocks):
        if b > 1:
            state_loads[b].wait()
            stage_values(b)
        stage_faces(b)
        residual = (first, second)[b] if b < 2 else residual_of(0, b)
        add_block(0, b, weigh(0, b, residual))
    send_rows(0)
    jac_loads[1].wait()
    for b in range(blocks):
        add_block(1, b, weigh(1, b, residual_of(1, b)))
        if b == 0:
            make_choose()
        if b == min(1, blocks - 1):
            send_sums(0)
    send_rows(1)
    send_sums(1)
    columns = []
    for part, pairs in enumerate(PARTS):
        for peer, source in plane_peers:
            sum_copy(part, peer, source).wait_recv()
        span = slice(pair_start[part], pair_start[part] + len(pairs))
        total = functools.reduce(jnp.add, [sums_in[source, span] for source in range(targets)])
        total = jnp.abs(total).reshape(len(pairs) * GROUP_ROWS, LANES)
        if part == 0:
            flag_ref[0, 0] = jnp.where(jnp.max(total[GROUP_ROWS - 1 : GROUP_ROWS]) > 0.0, 1, 0)
        pad = jnp.zeros((LANES - len(pairs) * GROUP_ROWS, LANES), jnp.float32)
        turned = jnp.concatenate([total, pad], axis=0).T
        for p, pair in enumerate(pairs):
            for side in range(len(pair)):
                columns.append(
                    turned[side * PATCH_DEV : (side + 1) * PATCH_DEV, p * GROUP_ROWS : p * GROUP_ROWS + PER_VAR]
                )
    out_ref[...] = jnp.concatenate(columns, axis=1)

    for copy in rims:
        copy.wait_send()
    for peer, source in z_peers:
        ids_copy(peer, z).wait_send()
    for part in range(len(PARTS)):
        for peer, source in z_peers:
            gather_copy(part, peer, z).wait_send()
        for peer, source in plane_peers:
            sum_copy(part, peer, me).wait_send()


def per_device(trace_azimuth, trace_radial, state, jacobian, lift_map, order, patch):
    face_len, rows_azi, rows_rad = trace_azimuth.shape
    kmax = jacobian.shape[0]
    n_azi, n_rad = lax.axis_size("azi"), lax.axis_size("rad")
    n_seat = SEATS if n_azi % SEATS == 0 else 1
    n_z, targets = n_azi // n_seat, n_seat * n_rad
    blocks = rows_azi // ROWS
    width = ROWS * LANES
    pairs = sum(len(part) for part in PARTS)
    f32, b16 = jnp.float32, jnp.bfloat16
    out, uneven = pl.pallas_call(
        functools.partial(fused_kernel, n_z, n_seat, n_rad),
        out_shape=(jax.ShapeDtypeStruct((PATCH_DEV, GROUPS), f32), jax.ShapeDtypeStruct((1, 1), jnp.int32)),
        in_specs=[pl.BlockSpec(memory_space=pl.ANY)] * 7,
        out_specs=(pl.BlockSpec(memory_space=pltpu.VMEM), pl.BlockSpec(memory_space=pltpu.SMEM)),
        scratch_shapes=[
            pltpu.VMEM(trace_azimuth.shape, b16),
            pltpu.VMEM(trace_radial.shape, b16),
            pltpu.VMEM((blocks, kmax, ROWS, LANES), b16),
            pltpu.VMEM(jacobian.shape, b16),
            pltpu.VMEM(lift_map.shape[::-1], b16),
            pltpu.VMEM(lift_map.shape, b16),
            pltpu.VMEM(order.shape, jnp.int32),
            pltpu.VMEM(patch.shape, jnp.int32),
            pltpu.VMEM((blocks, kmax, width), b16),
            pltpu.VMEM((blocks, 4 * face_len, width), b16),
            pltpu.VMEM((rows_azi // BAND, kmax, LANES), f32),
            pltpu.VMEM((face_len, rows_azi * LANES), b16),
            pltpu.VMEM((2, face_len, LANES), b16),
            pltpu.VMEM((2, face_len, LANES), b16),
            pltpu.VMEM((RUN_SLOTS, LANES), f32),
            pltpu.VMEM((n_z, RUN_SLOTS, LANES), f32),
            pltpu.VMEM((rows_azi // BAND * 2 * LANES, LANES), b16),
            pltpu.VMEM((n_z * 2 * RUN_SLOTS, targets * LANES), b16),
            pltpu.VMEM((pairs, GROUP_ROWS, LANES), f32),
            pltpu.VMEM((n_z, pairs, GROUP_ROWS, LANES), f32),
            pltpu.VMEM((targets, pairs, GROUP_ROWS, LANES), f32),
            pltpu.VMEM((targets, pairs, GROUP_ROWS, LANES), f32),
            pltpu.SemaphoreType.DMA((5 + len(PARTS),)),
            pltpu.SemaphoreType.DMA((blocks,)),
            pltpu.SemaphoreType.DMA((2, 2)),
            pltpu.SemaphoreType.DMA((2, n_z)),
            pltpu.SemaphoreType.DMA((2, len(PARTS), n_z)),
            pltpu.SemaphoreType.DMA((2, len(PARTS), targets)),
        ],
        compiler_params=pltpu.CompilerParams(collective_id=0, has_side_effects=True, vmem_limit_bytes=VLIM),
        cost_estimate=pl.CostEstimate(
            flops=2 * kmax * (kmax + 4 * face_len) * rows_azi * rows_rad,
            bytes_accessed=2 * kmax * rows_azi * rows_rad, transcendentals=0,
        ),
    )(trace_azimuth, trace_radial, state, jacobian, lift_map.T, order, patch)
    arguments = (trace_azimuth, trace_radial, state, jacobian, lift_map, order, patch)
    return lax.cond(uneven[0, 0] != 0, general_path, lambda *unused: out, *arguments)


def solution(mesh):
    in_specs = (
        P(None, "azi", "rad"),
        P(None, "azi", "rad"),
        P(None, "azi", "rad"),
        P(),
        P(),
        P("azi", "rad"),
        P("azi", "rad"),
    )
    out_specs = P(("azi", "rad"), None)
    return jax.shard_map(
        per_device, mesh=mesh, in_specs=in_specs, out_specs=out_specs, check_vma=False
    )
```

```python
import functools

import jax
import jax.numpy as jnp
import numpy as np
from jax import lax
from jax.experimental import pallas as pl
from jax.experimental.pallas import tpu as pltpu
from jax.sharding import PartitionSpec as P

DEG = 6
MODES = 216
KMAX = 1080
GROUPS = 90
PATCH_DEV = 48
BAND = 16
ROWS = 8
LANES = 128
SLOTS = 56
ID_LANE = LANES - 1
SUBS = 1
VLIM_RIM = 57 * 1024 * 1024
VLIM_MAIN = 57 * 1024 * 1024
SEATS = 2
DIRS = 3
VARS = 5
PER_VAR = DIRS * DEG
GROUP_ROWS = 24
RUN_SLOTS = 64
FLAG_SLOT = RUN_SLOTS - 1
DEPTH = 256
VLIM = 57 * 1024 * 1024
PARTS = (((0, 1), (2,)), ((3, 4),))
MESH_ID = pl.DeviceIdType.MESH


def rim_kernel(n_azi, n_rad, ta_ref, tr_ref, rim_a_ref, rim_r_ref, outgoing, recv, send_sem, recv_sem):
    azi, rad = lax.axis_index("azi"), lax.axis_index("rad")
    mesh_id = pl.DeviceIdType.MESH
    barrier = pltpu.get_barrier_semaphore()

    def towards(by_azi, by_rad):
        return {"azi": (azi + n_azi + by_azi) % n_azi, "rad": (rad + n_rad + by_rad) % n_rad}

    pl.semaphore_signal(barrier, inc=1, device_id=towards(-1, 0), device_id_type=mesh_id)
    pl.semaphore_signal(barrier, inc=1, device_id=towards(0, -1), device_id_type=mesh_id)

    outgoing[0] = ta_ref[:, ta_ref.shape[1] - 1, :]
    face_len, rows_azi, lanes = tr_ref.shape
    flat = tr_ref[...].reshape(face_len, rows_azi * lanes)
    lane = lax.broadcasted_iota(jnp.int32, (face_len, lanes), 1)
    column = jnp.zeros((face_len, lanes), jnp.float32)
    for i in range(rows_azi):
        piece = flat[:, i * lanes : (i + 1) * lanes].astype(jnp.float32)
        column = jnp.where(lane == i, pltpu.roll(piece, (i + 1) % lanes, 1), column)
    outgoing[1] = column.astype(jnp.bfloat16)

    pl.semaphore_wait(barrier, 2)
    copies = []
    for slot, target in enumerate((towards(1, 0), towards(0, 1))):
        copies.append(
            pltpu.make_async_remote_copy(
                src_ref=outgoing.at[slot], dst_ref=recv.at[slot],
                send_sem=send_sem.at[slot], recv_sem=recv_sem.at[slot],
                device_id=target, device_id_type=mesh_id,
            )
        )
    for copy in copies:
        copy.start()
    for copy in copies:
        copy.wait()
    rim_a_ref[...] = recv[0]
    rim_r_ref[...] = jnp.where(rad > 0, recv[1], jnp.zeros_like(recv[1]))


def mode_tables():
    mode_index = np.arange(KMAX)
    variable = mode_index // MODES
    inside = mode_index % MODES
    degrees = [inside // (DEG * DEG), inside // DEG % DEG, inside % DEG]
    lower_modes = np.maximum(np.maximum(degrees[0], degrees[1]), degrees[2]) <= DEG - 2
    group_index = np.arange(LANES)
    group_table = np.zeros((LANES, KMAX), np.float32)
    for direction in range(3):
        target = variable * 3 * DEG + direction * DEG + degrees[direction]
        group_table = group_table + (group_index[:, None] == target[None, :]).astype(np.float32)
    return (lower_modes, group_table)


def halves(value):
    high = value.astype(jnp.bfloat16)
    low = (value - high.astype(jnp.float32)).astype(jnp.bfloat16)
    return high, low


def exact_table_dot(table, value):
    high, low = halves(value)
    dims = (((1,), (1,)), ((), ()))
    return lax.dot_general(table, high, dims, preferred_element_type=jnp.float32) + lax.dot_general(
        table, low, dims, preferred_element_type=jnp.float32
    )


def slot_ids_of_runs(patch, rows_azi):
    slot = lax.broadcasted_iota(jnp.int32, (SLOTS, LANES), 0).astype(jnp.float32)
    upto = lax.broadcasted_iota(jnp.int32, (LANES, LANES), 0) <= lax.broadcasted_iota(
        jnp.int32, (LANES, LANES), 1
    )
    used = jnp.zeros((1, 1), jnp.float32)
    ids = jnp.zeros((SLOTS, 1), jnp.float32)
    for band in range(0, rows_azi, BAND):
        row = patch[band : band + 8].astype(jnp.float32)
        lane = lax.broadcasted_iota(jnp.int32, row.shape, 1)
        start = jnp.where((lane == 0) | (row != pltpu.roll(row, 1, 1)), 1.0, 0.0)
        rank = jnp.dot(
            start.astype(jnp.bfloat16), upto.astype(jnp.bfloat16), preferred_element_type=jnp.float32
        )
        mine = (slot == rank[:1] - 1.0 + used) & (start[:1] > 0.0)
        ids = ids + jnp.sum(jnp.where(mine, row[:1] + 1.0, 0.0), axis=1, keepdims=True)
        used = used + jnp.sum(start[:1], axis=1, keepdims=True)
    return ids.astype(jnp.int32) - 1


def local_kernel(
    ta_ref, tr_ref, st_ref, jac_ref, lift_ref, order_ref, patch_ref, lower_ref, table_ref,
    rim_a_ref, rim_r_ref, out_ref, carry, acc, lift, slots, jac, jac_sem,
):
    step = pl.program_id(0)
    fetch = pltpu.make_async_copy(jac_ref, jac, jac_sem)

    @pl.when(step == 0)
    def _():
        fetch.start()

    width = ROWS * LANES
    rows_azi = patch_ref.shape[0]
    face_len = ta_ref.shape[0]
    steps_band = BAND // ROWS

    all_patch = patch_ref[...]
    differ = jnp.int32(0)
    for band in range(0, rows_azi, BAND):
        rows = all_patch[band : band + BAND]
        differ = jnp.maximum(differ, jnp.max((rows != rows[:1]).astype(jnp.int32)))

    @pl.when(step == 0)
    def _():
        carry[...] = rim_a_ref[...]
        out_ref[...] = jnp.zeros_like(out_ref)
        lift[...] = lift_ref[...].T
        slots[...] = jnp.broadcast_to(slot_ids_of_runs(all_patch, rows_azi), slots.shape)

    @pl.when((step == 0) & (differ != 0))
    def _():
        none = jnp.int32(2**30)
        where_slot = lax.broadcasted_iota(jnp.int32, slots.shape, 0)

        def next_id(slot, last):
            found = jnp.min(jnp.where(all_patch > last, all_patch, none))
            slots[...] = jnp.where(where_slot == slot, jnp.where(found == none, -1, found), slots[...])
            return found

        lax.fori_loop(0, SLOTS, next_id, jnp.int32(-1))

    ta = ta_ref[...].reshape(face_len, width)
    tr = tr_ref[...].reshape(face_len, width)
    behind_a = jnp.concatenate([carry[...], ta[:, : width - LANES]], axis=1)
    carry[...] = ta[:, width - LANES :]
    row_id = lax.broadcasted_iota(jnp.int32, (rows_azi, width), 0)
    lane_id = lax.broadcasted_iota(jnp.int32, (rows_azi, width), 1)
    spread = ((row_id - step * ROWS) * LANES == lane_id).astype(jnp.bfloat16)
    rim = jnp.dot(rim_r_ref[:, :rows_azi], spread, preferred_element_type=jnp.float32)
    moved = pltpu.roll(tr.astype(jnp.float32), 1, 1)
    first = lax.broadcasted_iota(jnp.int32, (face_len, width), 1) % LANES == 0
    behind_r = jnp.where(first, rim, moved).astype(jnp.bfloat16)
    faces = jnp.concatenate([ta, behind_a, tr, behind_r], axis=0)

    @pl.when(step == 0)
    def _():
        fetch.wait()

    flags = (order_ref[...] == DEG - 1).astype(jnp.float32)
    sub = ROWS // SUBS

    def product_rows(index):
        span = slice(index * sub, (index + 1) * sub)
        cut = slice(index * sub * LANES, (index + 1) * sub * LANES)
        keep = jnp.maximum(lower_ref[...], flags[span].reshape(1, sub * LANES))
        values = st_ref[:, span, :].reshape(KMAX, sub * LANES) * keep.astype(jnp.bfloat16)
        adjoint = jnp.dot(lift[...], faces[:, cut], preferred_element_type=jnp.float32)
        residual = jnp.dot(jac[...], values, preferred_element_type=jnp.float32)
        product = adjoint * residual * keep
        return [product[:, row * LANES : (row + 1) * LANES] for row in range(sub)]

    band_start = pl.multiple_of(step // steps_band * BAND, BAND)
    band_row = patch_ref[pl.ds(band_start, 1), :]
    mine = patch_ref[pl.ds(pl.multiple_of(step * ROWS, ROWS), ROWS), :]
    place = slots[...]

    def add_to_patches(columns, row):
        grouped = exact_grouped(columns)
        chosen = (place == row).astype(jnp.bfloat16)
        out_ref[...] += exact_table_dot(chosen, grouped)

    def exact_grouped(columns):
        both = jnp.concatenate(halves(columns), axis=1)
        sums = jnp.dot(table_ref[...], both, preferred_element_type=jnp.float32)
        return sums[:, :LANES] + sums[:, LANES:]

    @pl.when(step % steps_band == 0)
    def _():
        acc[...] = jnp.zeros_like(acc)

    @pl.when(differ == 0)
    def _():
        for index in range(SUBS):
            acc[...] += functools.reduce(jnp.add, product_rows(index))

    @pl.when(differ != 0)
    def _():
        for index in range(SUBS):
            for row, product in enumerate(product_rows(index), index * sub):
                add_to_patches(product, mine[row : row + 1])

    @pl.when(step % steps_band == steps_band - 1)
    def _():
        @pl.when(differ == 0)
        def _():
            add_to_patches(acc[...], band_row)

    @pl.when(step == pl.num_programs(0) - 1)
    def _():
        lane = lax.broadcasted_iota(jnp.int32, out_ref.shape, 1)
        out_ref[...] = jnp.where(lane == ID_LANE, place.astype(jnp.float32), out_ref[...])


def exchange_kernel(
    n_z, n_seat, n_rad, rows_ref, out_ref, gathered, outgoing, recv,
    gather_send, gather_recv, sum_send, sum_recv,
):
    azi, rad = lax.axis_index("azi"), lax.axis_index("rad")
    z, seat = azi // n_seat, azi % n_seat
    targets = n_seat * n_rad
    me = seat * n_rad + rad
    mesh_id = pl.DeviceIdType.MESH

    def at_z(peer):
        return {"azi": peer * n_seat + seat, "rad": rad}

    def at_target(peer):
        return {"azi": z * n_seat + peer // n_rad, "rad": peer % n_rad}

    barrier = pltpu.get_barrier_semaphore()
    for k in range(1, n_z):
        pl.semaphore_signal(barrier, inc=1, device_id=at_z((z + k) % n_z), device_id_type=mesh_id)
    for k in range(1, targets):
        pl.semaphore_signal(
            barrier, inc=1, device_id=at_target((me + k) % targets), device_id_type=mesh_id
        )
    pl.semaphore_wait(barrier, n_z + targets - 2)

    def gather_copy(peer, source):
        return pltpu.make_async_remote_copy(
            src_ref=rows_ref, dst_ref=gathered.at[source],
            send_sem=gather_send.at[peer], recv_sem=gather_recv.at[source],
            device_id=at_z(peer), device_id_type=mesh_id,
        )

    def sum_copy(peer, source):
        return pltpu.make_async_remote_copy(
            src_ref=outgoing.at[peer], dst_ref=recv.at[source],
            send_sem=sum_send.at[peer], recv_sem=sum_recv.at[source],
            device_id=at_target(peer), device_id_type=mesh_id,
        )

    for k in range(1, n_z):
        gather_copy((z + k) % n_z, z).start()
    gathered[z] = rows_ref[...]
    for k in range(1, n_z):
        gather_copy((z + k) % n_z, (z + n_z - k) % n_z).wait_recv()

    rows = gathered[...].reshape(n_z * SLOTS, LANES)
    pick = (lax.broadcasted_iota(jnp.int32, (8, LANES), 1) == ID_LANE).astype(jnp.bfloat16)
    ids = exact_table_dot(pick, rows)[:1]
    count = targets * PATCH_DEV
    wanted = (z * count + lax.broadcasted_iota(jnp.int32, (count, n_z * SLOTS), 0)).astype(jnp.float32)
    chosen = (wanted == ids).astype(jnp.bfloat16)
    both = jnp.dot(
        chosen, jnp.concatenate(halves(rows), axis=1), preferred_element_type=jnp.float32
    )
    outgoing[...] = (both[:, :LANES] + both[:, LANES:]).reshape(targets, PATCH_DEV, LANES)

    for k in range(1, targets):
        sum_copy((me + k) % targets, me).start()
    total = outgoing[me]
    for k in range(1, targets):
        source = (me + targets - k) % targets
        sum_copy((me + k) % targets, source).wait_recv()
        total = total + recv[source]
    for k in range(1, n_z):
        gather_copy((z + k) % n_z, z).wait_send()
    for k in range(1, targets):
        sum_copy((me + k) % targets, me).wait_send()
    out_ref[...] = jnp.abs(total)[:, : out_ref.shape[1]]


def general_path(trace_azimuth, trace_radial, state, jacobian, lift_map, order, patch):
    face_len, rows_azi, rows_rad = trace_azimuth.shape
    n_azi, n_rad = lax.axis_size("azi"), lax.axis_size("rad")
    n_seat = SEATS if n_azi % SEATS == 0 else 1
    n_z, targets = n_azi // n_seat, n_seat * n_rad
    rim = jax.ShapeDtypeStruct((face_len, LANES), jnp.bfloat16)
    rim_azimuth, rim_radial = pl.pallas_call(
        functools.partial(rim_kernel, n_azi, n_rad),
        grid=(1,),
        out_shape=(rim, rim),
        in_specs=[
            pl.BlockSpec((face_len, ROWS, LANES), lambda t: (0, rows_azi // ROWS - 1, 0)),
            pl.BlockSpec(trace_radial.shape, lambda t: (0, 0, 0)),
        ],
        out_specs=(pl.BlockSpec(rim.shape, lambda t: (0, 0)),) * 2,
        scratch_shapes=[
            pltpu.VMEM((2,) + rim.shape, jnp.bfloat16),
            pltpu.VMEM((2,) + rim.shape, jnp.bfloat16),
            pltpu.SemaphoreType.DMA((2,)),
            pltpu.SemaphoreType.DMA((2,)),
        ],
        compiler_params=pltpu.CompilerParams(
            collective_id=2, has_side_effects=True, vmem_limit_bytes=VLIM_RIM
        ),
        cost_estimate=pl.CostEstimate(flops=0, bytes_accessed=12_000_000, transcendentals=0),
    )(trace_azimuth, trace_radial)
    lower_np, group_np = mode_tables()
    lower = jnp.asarray(lower_np.astype(np.float32)[:, None])
    table = jnp.asarray(group_np, jnp.bfloat16)

    def whole(shape):
        return pl.BlockSpec(shape, lambda t: (0,) * len(shape))

    def part(depth):
        return pl.BlockSpec((depth, ROWS, LANES), lambda t: (0, t, 0))

    rows = pl.pallas_call(
        local_kernel,
        grid=(rows_azi // ROWS,),
        out_shape=jax.ShapeDtypeStruct((SLOTS, LANES), jnp.float32),
        in_specs=[
            part(face_len), part(face_len), part(KMAX),
            pl.BlockSpec(memory_space=pl.ANY), whole(lift_map.shape[::-1]),
            pl.BlockSpec((ROWS, LANES), lambda t: (t, 0)), whole(patch.shape),
            whole(lower.shape), whole(table.shape),
            whole(rim_azimuth.shape), whole(rim_radial.shape),
        ],
        out_specs=whole((SLOTS, LANES)),
        scratch_shapes=[
            pltpu.VMEM((face_len, LANES), jnp.bfloat16),
            pltpu.VMEM((KMAX, LANES), jnp.float32),
            pltpu.VMEM(lift_map.shape, jnp.bfloat16),
            pltpu.VMEM((SLOTS, LANES), jnp.int32),
            pltpu.VMEM(jacobian.shape, jnp.bfloat16),
            pltpu.SemaphoreType.DMA,
        ],
        compiler_params=pltpu.CompilerParams(
            dimension_semantics=("arbitrary",), vmem_limit_bytes=VLIM_MAIN
        ),
        cost_estimate=pl.CostEstimate(
            flops=2 * KMAX * (KMAX + 4 * face_len) * rows_azi * rows_rad,
            bytes_accessed=2 * KMAX * rows_azi * rows_rad, transcendentals=0,
        ),
    )(trace_azimuth, trace_radial, state, jacobian, lift_map.T, order, patch, lower, table,
      rim_azimuth, rim_radial)

    return pl.pallas_call(
        functools.partial(exchange_kernel, n_z, n_seat, n_rad),
        out_shape=jax.ShapeDtypeStruct((PATCH_DEV, GROUPS), jnp.float32),
        in_specs=[pl.BlockSpec(memory_space=pltpu.VMEM)],
        out_specs=pl.BlockSpec(memory_space=pltpu.VMEM),
        scratch_shapes=[
            pltpu.VMEM((n_z, SLOTS, LANES), jnp.float32),
            pltpu.VMEM((targets, PATCH_DEV, LANES), jnp.float32),
            pltpu.VMEM((targets, PATCH_DEV, LANES), jnp.float32),
            pltpu.SemaphoreType.DMA((n_z,)),
            pltpu.SemaphoreType.DMA((n_z,)),
            pltpu.SemaphoreType.DMA((targets,)),
            pltpu.SemaphoreType.DMA((targets,)),
        ],
        compiler_params=pltpu.CompilerParams(collective_id=1, has_side_effects=True),
    )(rows)


def iota(shape, dim):
    return lax.broadcasted_iota(jnp.int32, shape, dim)


def float_halves(value):
    high = value.astype(jnp.bfloat16).astype(jnp.float32)
    return high, value - high


def table_dot(value, table):
    rows = value.shape[0]
    both = jnp.concatenate(float_halves(value), axis=0).astype(jnp.bfloat16)
    sums = jnp.dot(both, table, preferred_element_type=jnp.float32)
    return sums[:rows] + sums[rows:]


def group_table():
    group = iota((GROUP_ROWS, MODES), 0)
    mode = iota((GROUP_ROWS, MODES), 1)
    direction, degree = group // DEG, group % DEG
    of_mode = jnp.where(direction == 0, mode // (DEG * DEG), jnp.where(direction == 1, mode // DEG % DEG, mode % DEG))
    hit = (of_mode == degree) & (group < PER_VAR)
    return hit.astype(jnp.float32).astype(jnp.bfloat16)


def lower_modes():
    mode = iota((MODES, LANES), 0)
    most = jnp.maximum(jnp.maximum(mode // (DEG * DEG), mode // DEG % DEG), mode % DEG)
    return (most <= DEG - 2).astype(jnp.float32)


def fused_kernel(
    n_z, n_seat, n_rad, ta_hbm, tr_hbm, st_hbm, jac_hbm, lift_hbm, order_hbm, patch_hbm, out_ref, flag_ref,
    ta, tr, st, jac, lift_t, lift, order, patch, values, faces, acc, flat_r,
    rim_out, rim_in, ids_out, ids_in, place, choose, rows_out, rows_in, sums_out, sums_in,
    load_sem, state_sem, rim_sem, ids_sem, gather_sem, sum_sem,
):
    azi, rad = lax.axis_index("azi"), lax.axis_index("rad")
    n_azi = n_z * n_seat
    z, seat = azi // n_seat, azi % n_seat
    targets = n_seat * n_rad
    me = seat * n_rad + rad
    face_len, rows_azi, _ = ta.shape
    kmax = jac.shape[0]
    blocks = rows_azi // ROWS
    bands = rows_azi // BAND
    width = ROWS * LANES

    def towards(by_azi, by_rad):
        return {"azi": (azi + n_azi + by_azi) % n_azi, "rad": (rad + n_rad + by_rad) % n_rad}

    def at_z(peer):
        return {"azi": peer * n_seat + seat, "rad": rad}

    def at_target(peer):
        return {"azi": z * n_seat + peer // n_rad, "rad": peer % n_rad}

    barrier = pltpu.get_barrier_semaphore()
    senders = [towards(-1, 0), towards(0, -1)]
    senders += [at_z((z + k) % n_z) for k in range(1, n_z)]
    senders += [at_target((me + k) % targets) for k in range(1, targets)]
    for device in senders:
        pl.semaphore_signal(barrier, inc=1, device_id=device, device_id_type=MESH_ID)

    spans = []
    first_var = 0
    for part in PARTS:
        count = sum(len(pair) for pair in part)
        spans.append((first_var * MODES, count * MODES))
        first_var += count

    loads = [
        pltpu.make_async_copy(order_hbm, order, load_sem.at[0]),
        pltpu.make_async_copy(patch_hbm, patch, load_sem.at[1]),
        pltpu.make_async_copy(tr_hbm, tr, load_sem.at[2]),
        pltpu.make_async_copy(ta_hbm, ta, load_sem.at[3]),
        pltpu.make_async_copy(lift_hbm, lift_t, load_sem.at[4]),
    ]
    jac_loads = [
        pltpu.make_async_copy(jac_hbm.at[pl.ds(start, count)], jac.at[pl.ds(start, count)], load_sem.at[5 + i])
        for i, (start, count) in enumerate(spans)
    ]
    state_loads = [
        pltpu.make_async_copy(st_hbm.at[:, pl.ds(b * ROWS, ROWS), :], st.at[b], state_sem.at[b])
        for b in range(blocks)
    ]
    for copy in loads + [state_loads[0], jac_loads[0]]:
        copy.start()

    loads[2].wait()
    flat_r[...] = tr[...].reshape(face_len, rows_azi * LANES)
    lane = iota((face_len, LANES), 1)
    column = jnp.zeros((face_len, LANES), jnp.float32)
    for i in range(rows_azi):
        piece = flat_r[:, i * LANES : (i + 1) * LANES].astype(jnp.float32)
        column = jnp.where(lane == i, pltpu.roll(piece, (i + 1) % LANES, 1), column)
    rim_out[1] = column.astype(jnp.bfloat16)
    loads[3].wait()
    rim_out[0] = ta[:, rows_azi - 1, :]

    loads[0].wait()
    loads[1].wait()
    upto = (iota((LANES, LANES), 0) <= iota((LANES, LANES), 1)).astype(jnp.float32).astype(jnp.bfloat16)
    since = iota((LANES, LANES), 1) <= iota((LANES, LANES), 0)
    ones = jnp.ones((LANES, LANES), jnp.bfloat16)
    used = jnp.zeros((1, LANES), jnp.float32)
    ids = jnp.zeros((RUN_SLOTS, 1), jnp.float32)
    slot = iota((RUN_SLOTS, LANES), 0).astype(jnp.float32)
    slot_of = []
    for band in range(bands):
        row = patch[band * BAND : band * BAND + ROWS].astype(jnp.float32)
        start = jnp.where((iota(row.shape, 1) == 0) | (row != pltpu.roll(row, 1, 1)), 1.0, 0.0)
        rank_row = jnp.dot(start.astype(jnp.bfloat16), upto, preferred_element_type=jnp.float32)[:1] - 1.0 + used
        begun = jnp.where(since, start[:1], 0.0).astype(jnp.bfloat16)
        rank_col = jnp.dot(begun, ones, preferred_element_type=jnp.float32)
        mine = (slot == rank_row) & (start[:1] > 0.0)
        ids = ids + jnp.sum(jnp.where(mine, row[:1] + 1.0, 0.0), axis=1, keepdims=True)
        slot_of.append(rank_col - 1.0 + used)
        used = used + rank_col[LANES - 1 :]
    differ = jnp.zeros((1, 1), jnp.float32)
    for band in range(bands):
        rows = patch[band * BAND : (band + 1) * BAND]
        uneven = jnp.max((rows != rows[:1]).astype(jnp.float32), axis=0, keepdims=True)
        differ = jnp.maximum(differ, jnp.max(uneven, axis=1, keepdims=True))
    slot_id = jnp.broadcast_to(ids - 1.0, ids_out.shape)
    ids_out[...] = jnp.where(slot == float(FLAG_SLOT), -1.0 - differ, slot_id)
    ids_in[z] = ids_out[...]

    slot_lane = iota((LANES, LANES), 1).astype(jnp.float32)
    for side in range(2):
        for band in range(bands):
            begin = (side * bands + band) * LANES
            hit = slot_of[band] == slot_lane - float(side * RUN_SLOTS)
            place[begin : begin + LANES] = hit.astype(jnp.float32).astype(jnp.bfloat16)

    def rim_copy(which, target):
        return pltpu.make_async_remote_copy(
            src_ref=rim_out.at[which], dst_ref=rim_in.at[which],
            send_sem=rim_sem.at[0, which], recv_sem=rim_sem.at[1, which],
            device_id=target, device_id_type=MESH_ID,
        )

    def ids_copy(peer, source):
        return pltpu.make_async_remote_copy(
            src_ref=ids_out, dst_ref=ids_in.at[source],
            send_sem=ids_sem.at[0, peer], recv_sem=ids_sem.at[1, source],
            device_id=at_z(peer), device_id_type=MESH_ID,
        )

    def gather_copy(part, peer, source):
        span = pl.ds(pair_start[part], len(PARTS[part]))
        return pltpu.make_async_remote_copy(
            src_ref=rows_out.at[span], dst_ref=rows_in.at[source, span],
            send_sem=gather_sem.at[0, part, peer], recv_sem=gather_sem.at[1, part, source],
            device_id=at_z(peer), device_id_type=MESH_ID,
        )

    def sum_copy(part, peer, source):
        span = pl.ds(pair_start[part], len(PARTS[part]))
        return pltpu.make_async_remote_copy(
            src_ref=sums_out.at[peer, span], dst_ref=sums_in.at[source, span],
            send_sem=sum_sem.at[0, part, peer], recv_sem=sum_sem.at[1, part, source],
            device_id=at_target(peer), device_id_type=MESH_ID,
        )

    pair_start = [sum(len(part) for part in PARTS[:i]) for i in range(len(PARTS))]
    z_peers = [((z + k) % n_z, (z + n_z - k) % n_z) for k in range(1, n_z)]
    plane_peers = [((me + k) % targets, (me + targets - k) % targets) for k in range(1, targets)]

    pl.semaphore_wait(barrier, len(senders))
    rims = [rim_copy(0, towards(1, 0)), rim_copy(1, towards(0, 1))]
    for copy in rims:
        copy.start()
    for peer, source in z_peers:
        ids_copy(peer, z).start()

    loads[4].wait()
    lift[...] = lift_t[...].T
    lower = lower_modes()
    table = group_table()
    lower_all = jnp.concatenate([lower] * VARS, axis=0)
    lower_all_16 = lower_all.astype(jnp.bfloat16)

    def flag_row(row):
        return (order[row : row + 1] == DEG - 1).astype(jnp.float32)

    def stage_values(b):
        keep = jnp.concatenate(
            [jnp.maximum(lower_all_16, flag_row(b * ROWS + i).astype(jnp.bfloat16)) for i in range(ROWS)], axis=1
        )
        values[b] = st[b].reshape(kmax, width) * keep

    def stage_faces(b):
        ta_b = ta[:, b * ROWS : (b + 1) * ROWS, :].reshape(face_len, width)
        if b == 0:
            before = rim_in[0]
        else:
            before = ta[:, b * ROWS - 1, :]
        tr_b = flat_r[:, b * width : (b + 1) * width]
        rim = rim_in[1].astype(jnp.float32)
        pieces = []
        for i in range(ROWS):
            moved = pltpu.roll(tr_b[:, i * LANES : (i + 1) * LANES].astype(jnp.float32), 1, 1)
            row = b * ROWS + i
            edge = pltpu.roll(rim, (LANES - row) % LANES, 1)
            pieces.append(jnp.where(lane == 0, jnp.where(rad > 0, edge, 0.0), moved).astype(jnp.bfloat16))
        faces[b, 0:face_len] = ta_b
        faces[b, face_len : 2 * face_len] = jnp.concatenate([before, ta_b[:, : width - LANES]], axis=1)
        faces[b, 2 * face_len : 3 * face_len] = tr_b
        faces[b, 3 * face_len :] = jnp.concatenate(pieces, axis=1)

    def weigh(part, b, residual):
        start, count = spans[part]
        adjoint = jnp.dot(lift[start : start + count], faces[b], preferred_element_type=jnp.float32)
        low = lower_all[start : start + count]
        total = None
        for i in range(ROWS):
            cut = slice(i * LANES, (i + 1) * LANES)
            term = adjoint[:, cut] * residual[:, cut] * jnp.maximum(low, flag_row(b * ROWS + i))
            total = term if total is None else total + term
        return total

    def residual_of(part, b):
        start, count = spans[part]
        return jnp.dot(jac[start : start + count], values[b], preferred_element_type=jnp.float32)

    def add_block(part, b, total):
        start, count = spans[part]
        band = b * ROWS // BAND
        if b * ROWS % BAND == 0:
            acc[band, start : start + count] = total
        else:
            acc[band, start : start + count] += total

    def send_rows(part):
        halves_of = []
        for var in [var for pair in PARTS[part] for var in pair]:
            for band in range(bands):
                halves_of += float_halves(acc[band, var * MODES : (var + 1) * MODES])
        both = jnp.concatenate(halves_of, axis=1).astype(jnp.bfloat16)
        sums = jnp.dot(table, both, preferred_element_type=jnp.float32)
        begin = 0
        for p, pair in enumerate(PARTS[part], pair_start[part]):
            terms = []
            for i in range(len(pair) * bands):
                at = begin + 2 * i * LANES
                terms.append(sums[:, at : at + LANES] + sums[:, at + LANES : at + 2 * LANES])
            begin += 2 * len(terms) * LANES
            rows_out[p] = table_dot(jnp.concatenate(terms, axis=1), place[: len(terms) * LANES])
        for peer, source in z_peers:
            gather_copy(part, peer, z).start()
        span = pl.ds(pair_start[part], len(PARTS[part]))
        rows_in[z, span] = rows_out[span]

    def send_sums(part):
        for peer, source in z_peers:
            gather_copy(part, peer, source).wait_recv()
        flags = [ids_in[peer, FLAG_SLOT : FLAG_SLOT + 1] for peer in range(n_z)]
        flag = -1.0 - functools.reduce(jnp.minimum, flags)
        for p in range(pair_start[part], pair_start[part] + len(PARTS[part])):
            terms = jnp.concatenate([rows_in[peer, p] for peer in range(n_z)], axis=1)
            sums = table_dot(terms, choose[...])
            for target in range(targets):
                piece = sums[:, target * LANES : (target + 1) * LANES]
                if p == 0:
                    piece = jnp.where(iota(piece.shape, 0) == GROUP_ROWS - 1, flag, piece)
                sums_out[target, p] = piece
        for peer, source in plane_peers:
            sum_copy(part, peer, me).start()
        span = pl.ds(pair_start[part], len(PARTS[part]))
        sums_in[me, span] = sums_out[me, span]

    def make_choose():
        for peer, source in z_peers:
            ids_copy(peer, source).wait_recv()
        here = iota((1, LANES), 1)
        sides = []
        for side in range(2):
            inside = (here >= side * PATCH_DEV) & (here < (side + 1) * PATCH_DEV)
            sides.append(jnp.where(inside, here - side * PATCH_DEV, -(2**20)).astype(jnp.float32))
        base = (z * targets * PATCH_DEV).astype(jnp.float32)
        for peer in range(n_z):
            for side in range(2):
                begin = (2 * peer + side) * RUN_SLOTS
                for target in range(targets):
                    hit = ids_in[peer] == sides[side] + (base + float(target * PATCH_DEV))
                    choose[begin : begin + RUN_SLOTS, target * LANES : (target + 1) * LANES] = hit.astype(
                        jnp.float32
                    ).astype(jnp.bfloat16)

    state_loads[0].wait()
    for copy in state_loads[1:] + jac_loads[1:]:
        copy.start()
    stage_values(0)
    jac_loads[0].wait()
    first = residual_of(0, 0)
    state_loads[1].wait()
    stage_values(1)
    second = residual_of(0, 1)
    for copy in rims:
        copy.wait_recv()
    for b in range(blocks):
        if b > 1:
            state_loads[b].wait()
            stage_values(b)
        stage_faces(b)
        residual = (first, second)[b] if b < 2 else residual_of(0, b)
        add_block(0, b, weigh(0, b, residual))
    send_rows(0)
    jac_loads[1].wait()
    for b in range(blocks):
        add_block(1, b, weigh(1, b, residual_of(1, b)))
        if b == 0:
            make_choose()
        if b == min(1, blocks - 1):
            send_sums(0)
    send_rows(1)
    send_sums(1)
    columns = []
    for part, pairs in enumerate(PARTS):
        for peer, source in plane_peers:
            sum_copy(part, peer, source).wait_recv()
        span = slice(pair_start[part], pair_start[part] + len(pairs))
        total = functools.reduce(jnp.add, [sums_in[source, span] for source in range(targets)])
        total = jnp.abs(total).reshape(len(pairs) * GROUP_ROWS, LANES)
        if part == 0:
            flag_ref[0, 0] = jnp.where(jnp.max(total[GROUP_ROWS - 1 : GROUP_ROWS]) > 0.0, 1, 0)
        pad = jnp.zeros((LANES - len(pairs) * GROUP_ROWS, LANES), jnp.float32)
        turned = jnp.concatenate([total, pad], axis=0).T
        for p, pair in enumerate(pairs):
            for side in range(len(pair)):
                columns.append(
                    turned[side * PATCH_DEV : (side + 1) * PATCH_DEV, p * GROUP_ROWS : p * GROUP_ROWS + PER_VAR]
                )
    out_ref[...] = jnp.concatenate(columns, axis=1)

    for copy in rims:
        copy.wait_send()
    for peer, source in z_peers:
        ids_copy(peer, z).wait_send()
    for part in range(len(PARTS)):
        for peer, source in z_peers:
            gather_copy(part, peer, z).wait_send()
        for peer, source in plane_peers:
            sum_copy(part, peer, me).wait_send()


def per_device(trace_azimuth, trace_radial, state, jacobian, lift_map, order, patch):
    face_len, rows_azi, rows_rad = trace_azimuth.shape
    kmax = jacobian.shape[0]
    n_azi, n_rad = lax.axis_size("azi"), lax.axis_size("rad")
    n_seat = SEATS if n_azi % SEATS == 0 else 1
    n_z, targets = n_azi // n_seat, n_seat * n_rad
    blocks = rows_azi // ROWS
    width = ROWS * LANES
    pairs = sum(len(part) for part in PARTS)
    f32, b16 = jnp.float32, jnp.bfloat16
    out, uneven = pl.pallas_call(
        functools.partial(fused_kernel, n_z, n_seat, n_rad),
        out_shape=(jax.ShapeDtypeStruct((PATCH_DEV, GROUPS), f32), jax.ShapeDtypeStruct((1, 1), jnp.int32)),
        in_specs=[pl.BlockSpec(memory_space=pl.ANY)] * 7,
        out_specs=(pl.BlockSpec(memory_space=pltpu.VMEM), pl.BlockSpec(memory_space=pltpu.SMEM)),
        scratch_shapes=[
            pltpu.VMEM(trace_azimuth.shape, b16),
            pltpu.VMEM(trace_radial.shape, b16),
            pltpu.VMEM((blocks, kmax, ROWS, LANES), b16),
            pltpu.VMEM(jacobian.shape, b16),
            pltpu.VMEM(lift_map.shape[::-1], b16),
            pltpu.VMEM(lift_map.shape, b16),
            pltpu.VMEM(order.shape, jnp.int32),
            pltpu.VMEM(patch.shape, jnp.int32),
            pltpu.VMEM((blocks, kmax, width), b16),
            pltpu.VMEM((blocks, 4 * face_len, width), b16),
            pltpu.VMEM((rows_azi // BAND, kmax, LANES), f32),
            pltpu.VMEM((face_len, rows_azi * LANES), b16),
            pltpu.VMEM((2, face_len, LANES), b16),
            pltpu.VMEM((2, face_len, LANES), b16),
            pltpu.VMEM((RUN_SLOTS, LANES), f32),
            pltpu.VMEM((n_z, RUN_SLOTS, LANES), f32),
            pltpu.VMEM((rows_azi // BAND * 2 * LANES, LANES), b16),
            pltpu.VMEM((n_z * 2 * RUN_SLOTS, targets * LANES), b16),
            pltpu.VMEM((pairs, GROUP_ROWS, LANES), f32),
            pltpu.VMEM((n_z, pairs, GROUP_ROWS, LANES), f32),
            pltpu.VMEM((targets, pairs, GROUP_ROWS, LANES), f32),
            pltpu.VMEM((targets, pairs, GROUP_ROWS, LANES), f32),
            pltpu.SemaphoreType.DMA((5 + len(PARTS),)),
            pltpu.SemaphoreType.DMA((blocks,)),
            pltpu.SemaphoreType.DMA((2, 2)),
            pltpu.SemaphoreType.DMA((2, n_z)),
            pltpu.SemaphoreType.DMA((2, len(PARTS), n_z)),
            pltpu.SemaphoreType.DMA((2, len(PARTS), targets)),
        ],
        compiler_params=pltpu.CompilerParams(collective_id=0, has_side_effects=True, vmem_limit_bytes=VLIM),
        cost_estimate=pl.CostEstimate(
            flops=2 * kmax * (kmax + 4 * face_len) * rows_azi * rows_rad,
            bytes_accessed=2 * kmax * rows_azi * rows_rad, transcendentals=0,
        ),
    )(trace_azimuth, trace_radial, state, jacobian, lift_map.T, order, patch)
    arguments = (trace_azimuth, trace_radial, state, jacobian, lift_map, order, patch)
    return lax.cond(uneven[0, 0] != 0, general_path, lambda *unused: out, *arguments)


def solution(mesh):
    in_specs = (
        P(None, "azi", "rad"),
        P(None, "azi", "rad"),
        P(None, "azi", "rad"),
        P(),
        P(),
        P("azi", "rad"),
        P("azi", "rad"),
    )
    out_specs = P(("azi", "rad"), None)
    return jax.shard_map(
        per_device, mesh=mesh, in_specs=in_specs, out_specs=out_specs, check_vma=False
    )
```

```python
import functools

import jax
import jax.numpy as jnp
import numpy as np
from jax import lax
from jax.experimental import pallas as pl
from jax.experimental.pallas import tpu as pltpu
from jax.sharding import PartitionSpec as P

DEG = 6
MODES = 216
KMAX = 1080
GROUPS = 90
PATCH_DEV = 48
BAND = 16
ROWS = 8
LANES = 128
SLOTS = 56
ID_LANE = LANES - 1
SUBS = 1
VLIM_RIM = 57 * 1024 * 1024
VLIM_MAIN = 57 * 1024 * 1024
SEATS = 2
DIRS = 3
VARS = 5
PER_VAR = DIRS * DEG
GROUP_ROWS = 24
RUN_SLOTS = 64
FLAG_SLOT = RUN_SLOTS - 1
DEPTH = 256
VLIM = 57 * 1024 * 1024
PARTS = (((0, 1), (2,)), ((3, 4),))
MESH_ID = pl.DeviceIdType.MESH


def rim_kernel(n_azi, n_rad, ta_ref, tr_ref, rim_a_ref, rim_r_ref, outgoing, recv, send_sem, recv_sem):
    azi, rad = lax.axis_index("azi"), lax.axis_index("rad")
    mesh_id = pl.DeviceIdType.MESH
    barrier = pltpu.get_barrier_semaphore()

    def towards(by_azi, by_rad):
        return {"azi": (azi + n_azi + by_azi) % n_azi, "rad": (rad + n_rad + by_rad) % n_rad}

    pl.semaphore_signal(barrier, inc=1, device_id=towards(-1, 0), device_id_type=mesh_id)
    pl.semaphore_signal(barrier, inc=1, device_id=towards(0, -1), device_id_type=mesh_id)

    outgoing[0] = ta_ref[:, ta_ref.shape[1] - 1, :]
    face_len, rows_azi, lanes = tr_ref.shape
    flat = tr_ref[...].reshape(face_len, rows_azi * lanes)
    lane = lax.broadcasted_iota(jnp.int32, (face_len, lanes), 1)
    column = jnp.zeros((face_len, lanes), jnp.float32)
    for i in range(rows_azi):
        piece = flat[:, i * lanes : (i + 1) * lanes].astype(jnp.float32)
        column = jnp.where(lane == i, pltpu.roll(piece, (i + 1) % lanes, 1), column)
    outgoing[1] = column.astype(jnp.bfloat16)

    pl.semaphore_wait(barrier, 2)
    copies = []
    for slot, target in enumerate((towards(1, 0), towards(0, 1))):
        copies.append(
            pltpu.make_async_remote_copy(
                src_ref=outgoing.at[slot], dst_ref=recv.at[slot],
                send_sem=send_sem.at[slot], recv_sem=recv_sem.at[slot],
                device_id=target, device_id_type=mesh_id,
            )
        )
    for copy in copies:
        copy.start()
    for copy in copies:
        copy.wait()
    rim_a_ref[...] = recv[0]
    rim_r_ref[...] = jnp.where(rad > 0, recv[1], jnp.zeros_like(recv[1]))


def mode_tables():
    mode_index = np.arange(KMAX)
    variable = mode_index // MODES
    inside = mode_index % MODES
    degrees = [inside // (DEG * DEG), inside // DEG % DEG, inside % DEG]
    lower_modes = np.maximum(np.maximum(degrees[0], degrees[1]), degrees[2]) <= DEG - 2
    group_index = np.arange(LANES)
    group_table = np.zeros((LANES, KMAX), np.float32)
    for direction in range(3):
        target = variable * 3 * DEG + direction * DEG + degrees[direction]
        group_table = group_table + (group_index[:, None] == target[None, :]).astype(np.float32)
    return (lower_modes, group_table)


def halves(value):
    high = value.astype(jnp.bfloat16)
    low = (value - high.astype(jnp.float32)).astype(jnp.bfloat16)
    return high, low


def exact_table_dot(table, value):
    high, low = halves(value)
    dims = (((1,), (1,)), ((), ()))
    return lax.dot_general(table, high, dims, preferred_element_type=jnp.float32) + lax.dot_general(
        table, low, dims, preferred_element_type=jnp.float32
    )


def slot_ids_of_runs(patch, rows_azi):
    slot = lax.broadcasted_iota(jnp.int32, (SLOTS, LANES), 0).astype(jnp.float32)
    upto = lax.broadcasted_iota(jnp.int32, (LANES, LANES), 0) <= lax.broadcasted_iota(
        jnp.int32, (LANES, LANES), 1
    )
    used = jnp.zeros((1, 1), jnp.float32)
    ids = jnp.zeros((SLOTS, 1), jnp.float32)
    for band in range(0, rows_azi, BAND):
        row = patch[band : band + 8].astype(jnp.float32)
        lane = lax.broadcasted_iota(jnp.int32, row.shape, 1)
        start = jnp.where((lane == 0) | (row != pltpu.roll(row, 1, 1)), 1.0, 0.0)
        rank = jnp.dot(
            start.astype(jnp.bfloat16), upto.astype(jnp.bfloat16), preferred_element_type=jnp.float32
        )
        mine = (slot == rank[:1] - 1.0 + used) & (start[:1] > 0.0)
        ids = ids + jnp.sum(jnp.where(mine, row[:1] + 1.0, 0.0), axis=1, keepdims=True)
        used = used + jnp.sum(start[:1], axis=1, keepdims=True)
    return ids.astype(jnp.int32) - 1


def local_kernel(
    ta_ref, tr_ref, st_ref, jac_ref, lift_ref, order_ref, patch_ref, lower_ref, table_ref,
    rim_a_ref, rim_r_ref, out_ref, carry, acc, lift, slots, jac, jac_sem,
):
    step = pl.program_id(0)
    fetch = pltpu.make_async_copy(jac_ref, jac, jac_sem)

    @pl.when(step == 0)
    def _():
        fetch.start()

    width = ROWS * LANES
    rows_azi = patch_ref.shape[0]
    face_len = ta_ref.shape[0]
    steps_band = BAND // ROWS

    all_patch = patch_ref[...]
    differ = jnp.int32(0)
    for band in range(0, rows_azi, BAND):
        rows = all_patch[band : band + BAND]
        differ = jnp.maximum(differ, jnp.max((rows != rows[:1]).astype(jnp.int32)))

    @pl.when(step == 0)
    def _():
        carry[...] = rim_a_ref[...]
        out_ref[...] = jnp.zeros_like(out_ref)
        lift[...] = lift_ref[...].T
        slots[...] = jnp.broadcast_to(slot_ids_of_runs(all_patch, rows_azi), slots.shape)

    @pl.when((step == 0) & (differ != 0))
    def _():
        none = jnp.int32(2**30)
        where_slot = lax.broadcasted_iota(jnp.int32, slots.shape, 0)

        def next_id(slot, last):
            found = jnp.min(jnp.where(all_patch > last, all_patch, none))
            slots[...] = jnp.where(where_slot == slot, jnp.where(found == none, -1, found), slots[...])
            return found

        lax.fori_loop(0, SLOTS, next_id, jnp.int32(-1))

    ta = ta_ref[...].reshape(face_len, width)
    tr = tr_ref[...].reshape(face_len, width)
    behind_a = jnp.concatenate([carry[...], ta[:, : width - LANES]], axis=1)
    carry[...] = ta[:, width - LANES :]
    row_id = lax.broadcasted_iota(jnp.int32, (rows_azi, width), 0)
    lane_id = lax.broadcasted_iota(jnp.int32, (rows_azi, width), 1)
    spread = ((row_id - step * ROWS) * LANES == lane_id).astype(jnp.bfloat16)
    rim = jnp.dot(rim_r_ref[:, :rows_azi], spread, preferred_element_type=jnp.float32)
    moved = pltpu.roll(tr.astype(jnp.float32), 1, 1)
    first = lax.broadcasted_iota(jnp.int32, (face_len, width), 1) % LANES == 0
    behind_r = jnp.where(first, rim, moved).astype(jnp.bfloat16)
    faces = jnp.concatenate([ta, behind_a, tr, behind_r], axis=0)

    @pl.when(step == 0)
    def _():
        fetch.wait()

    flags = (order_ref[...] == DEG - 1).astype(jnp.float32)
    sub = ROWS // SUBS

    def product_rows(index):
        span = slice(index * sub, (index + 1) * sub)
        cut = slice(index * sub * LANES, (index + 1) * sub * LANES)
        keep = jnp.maximum(lower_ref[...], flags[span].reshape(1, sub * LANES))
        values = st_ref[:, span, :].reshape(KMAX, sub * LANES) * keep.astype(jnp.bfloat16)
        adjoint = jnp.dot(lift[...], faces[:, cut], preferred_element_type=jnp.float32)
        residual = jnp.dot(jac[...], values, preferred_element_type=jnp.float32)
        product = adjoint * residual * keep
        return [product[:, row * LANES : (row + 1) * LANES] for row in range(sub)]

    band_start = pl.multiple_of(step // steps_band * BAND, BAND)
    band_row = patch_ref[pl.ds(band_start, 1), :]
    mine = patch_ref[pl.ds(pl.multiple_of(step * ROWS, ROWS), ROWS), :]
    place = slots[...]

    def add_to_patches(columns, row):
        grouped = exact_grouped(columns)
        chosen = (place == row).astype(jnp.bfloat16)
        out_ref[...] += exact_table_dot(chosen, grouped)

    def exact_grouped(columns):
        both = jnp.concatenate(halves(columns), axis=1)
        sums = jnp.dot(table_ref[...], both, preferred_element_type=jnp.float32)
        return sums[:, :LANES] + sums[:, LANES:]

    @pl.when(step % steps_band == 0)
    def _():
        acc[...] = jnp.zeros_like(acc)

    @pl.when(differ == 0)
    def _():
        for index in range(SUBS):
            acc[...] += functools.reduce(jnp.add, product_rows(index))

    @pl.when(differ != 0)
    def _():
        for index in range(SUBS):
            for row, product in enumerate(product_rows(index), index * sub):
                add_to_patches(product, mine[row : row + 1])

    @pl.when(step % steps_band == steps_band - 1)
    def _():
        @pl.when(differ == 0)
        def _():
            add_to_patches(acc[...], band_row)

    @pl.when(step == pl.num_programs(0) - 1)
    def _():
        lane = lax.broadcasted_iota(jnp.int32, out_ref.shape, 1)
        out_ref[...] = jnp.where(lane == ID_LANE, place.astype(jnp.float32), out_ref[...])


def exchange_kernel(
    n_z, n_seat, n_rad, rows_ref, out_ref, gathered, outgoing, recv,
    gather_send, gather_recv, sum_send, sum_recv,
):
    azi, rad = lax.axis_index("azi"), lax.axis_index("rad")
    z, seat = azi // n_seat, azi % n_seat
    targets = n_seat * n_rad
    me = seat * n_rad + rad
    mesh_id = pl.DeviceIdType.MESH

    def at_z(peer):
        return {"azi": peer * n_seat + seat, "rad": rad}

    def at_target(peer):
        return {"azi": z * n_seat + peer // n_rad, "rad": peer % n_rad}

    barrier = pltpu.get_barrier_semaphore()
    for k in range(1, n_z):
        pl.semaphore_signal(barrier, inc=1, device_id=at_z((z + k) % n_z), device_id_type=mesh_id)
    for k in range(1, targets):
        pl.semaphore_signal(
            barrier, inc=1, device_id=at_target((me + k) % targets), device_id_type=mesh_id
        )
    pl.semaphore_wait(barrier, n_z + targets - 2)

    def gather_copy(peer, source):
        return pltpu.make_async_remote_copy(
            src_ref=rows_ref, dst_ref=gathered.at[source],
            send_sem=gather_send.at[peer], recv_sem=gather_recv.at[source],
            device_id=at_z(peer), device_id_type=mesh_id,
        )

    def sum_copy(peer, source):
        return pltpu.make_async_remote_copy(
            src_ref=outgoing.at[peer], dst_ref=recv.at[source],
            send_sem=sum_send.at[peer], recv_sem=sum_recv.at[source],
            device_id=at_target(peer), device_id_type=mesh_id,
        )

    for k in range(1, n_z):
        gather_copy((z + k) % n_z, z).start()
    gathered[z] = rows_ref[...]
    for k in range(1, n_z):
        gather_copy((z + k) % n_z, (z + n_z - k) % n_z).wait_recv()

    rows = gathered[...].reshape(n_z * SLOTS, LANES)
    pick = (lax.broadcasted_iota(jnp.int32, (8, LANES), 1) == ID_LANE).astype(jnp.bfloat16)
    ids = exact_table_dot(pick, rows)[:1]
    count = targets * PATCH_DEV
    wanted = (z * count + lax.broadcasted_iota(jnp.int32, (count, n_z * SLOTS), 0)).astype(jnp.float32)
    chosen = (wanted == ids).astype(jnp.bfloat16)
    both = jnp.dot(
        chosen, jnp.concatenate(halves(rows), axis=1), preferred_element_type=jnp.float32
    )
    outgoing[...] = (both[:, :LANES] + both[:, LANES:]).reshape(targets, PATCH_DEV, LANES)

    for k in range(1, targets):
        sum_copy((me + k) % targets, me).start()
    total = outgoing[me]
    for k in range(1, targets):
        source = (me + targets - k) % targets
        sum_copy((me + k) % targets, source).wait_recv()
        total = total + recv[source]
    for k in range(1, n_z):
        gather_copy((z + k) % n_z, z).wait_send()
    for k in range(1, targets):
        sum_copy((me + k) % targets, me).wait_send()
    out_ref[...] = jnp.abs(total)[:, : out_ref.shape[1]]


def general_path(trace_azimuth, trace_radial, state, jacobian, lift_map, order, patch):
    face_len, rows_azi, rows_rad = trace_azimuth.shape
    n_azi, n_rad = lax.axis_size("azi"), lax.axis_size("rad")
    n_seat = SEATS if n_azi % SEATS == 0 else 1
    n_z, targets = n_azi // n_seat, n_seat * n_rad
    rim = jax.ShapeDtypeStruct((face_len, LANES), jnp.bfloat16)
    rim_azimuth, rim_radial = pl.pallas_call(
        functools.partial(rim_kernel, n_azi, n_rad),
        grid=(1,),
        out_shape=(rim, rim),
        in_specs=[
            pl.BlockSpec((face_len, ROWS, LANES), lambda t: (0, rows_azi // ROWS - 1, 0)),
            pl.BlockSpec(trace_radial.shape, lambda t: (0, 0, 0)),
        ],
        out_specs=(pl.BlockSpec(rim.shape, lambda t: (0, 0)),) * 2,
        scratch_shapes=[
            pltpu.VMEM((2,) + rim.shape, jnp.bfloat16),
            pltpu.VMEM((2,) + rim.shape, jnp.bfloat16),
            pltpu.SemaphoreType.DMA((2,)),
            pltpu.SemaphoreType.DMA((2,)),
        ],
        compiler_params=pltpu.CompilerParams(
            collective_id=2, has_side_effects=True, vmem_limit_bytes=VLIM_RIM
        ),
        cost_estimate=pl.CostEstimate(flops=0, bytes_accessed=12_000_000, transcendentals=0),
    )(trace_azimuth, trace_radial)
    lower_np, group_np = mode_tables()
    lower = jnp.asarray(lower_np.astype(np.float32)[:, None])
    table = jnp.asarray(group_np, jnp.bfloat16)

    def whole(shape):
        return pl.BlockSpec(shape, lambda t: (0,) * len(shape))

    def part(depth):
        return pl.BlockSpec((depth, ROWS, LANES), lambda t: (0, t, 0))

    rows = pl.pallas_call(
        local_kernel,
        grid=(rows_azi // ROWS,),
        out_shape=jax.ShapeDtypeStruct((SLOTS, LANES), jnp.float32),
        in_specs=[
            part(face_len), part(face_len), part(KMAX),
            pl.BlockSpec(memory_space=pl.ANY), whole(lift_map.shape[::-1]),
            pl.BlockSpec((ROWS, LANES), lambda t: (t, 0)), whole(patch.shape),
            whole(lower.shape), whole(table.shape),
            whole(rim_azimuth.shape), whole(rim_radial.shape),
        ],
        out_specs=whole((SLOTS, LANES)),
        scratch_shapes=[
            pltpu.VMEM((face_len, LANES), jnp.bfloat16),
            pltpu.VMEM((KMAX, LANES), jnp.float32),
            pltpu.VMEM(lift_map.shape, jnp.bfloat16),
            pltpu.VMEM((SLOTS, LANES), jnp.int32),
            pltpu.VMEM(jacobian.shape, jnp.bfloat16),
            pltpu.SemaphoreType.DMA,
        ],
        compiler_params=pltpu.CompilerParams(
            dimension_semantics=("arbitrary",), vmem_limit_bytes=VLIM_MAIN
        ),
        cost_estimate=pl.CostEstimate(
            flops=2 * KMAX * (KMAX + 4 * face_len) * rows_azi * rows_rad,
            bytes_accessed=2 * KMAX * rows_azi * rows_rad, transcendentals=0,
        ),
    )(trace_azimuth, trace_radial, state, jacobian, lift_map.T, order, patch, lower, table,
      rim_azimuth, rim_radial)

    return pl.pallas_call(
        functools.partial(exchange_kernel, n_z, n_seat, n_rad),
        out_shape=jax.ShapeDtypeStruct((PATCH_DEV, GROUPS), jnp.float32),
        in_specs=[pl.BlockSpec(memory_space=pltpu.VMEM)],
        out_specs=pl.BlockSpec(memory_space=pltpu.VMEM),
        scratch_shapes=[
            pltpu.VMEM((n_z, SLOTS, LANES), jnp.float32),
            pltpu.VMEM((targets, PATCH_DEV, LANES), jnp.float32),
            pltpu.VMEM((targets, PATCH_DEV, LANES), jnp.float32),
            pltpu.SemaphoreType.DMA((n_z,)),
            pltpu.SemaphoreType.DMA((n_z,)),
            pltpu.SemaphoreType.DMA((targets,)),
            pltpu.SemaphoreType.DMA((targets,)),
        ],
        compiler_params=pltpu.CompilerParams(collective_id=1, has_side_effects=True),
    )(rows)


def iota(shape, dim):
    return lax.broadcasted_iota(jnp.int32, shape, dim)


def float_halves(value):
    high = value.astype(jnp.bfloat16).astype(jnp.float32)
    return high, value - high


def table_dot(value, table):
    rows = value.shape[0]
    both = jnp.concatenate(float_halves(value), axis=0).astype(jnp.bfloat16)
    sums = jnp.dot(both, table, preferred_element_type=jnp.float32)
    return sums[:rows] + sums[rows:]


def group_table():
    group = iota((GROUP_ROWS, MODES), 0)
    mode = iota((GROUP_ROWS, MODES), 1)
    direction, degree = group // DEG, group % DEG
    of_mode = jnp.where(direction == 0, mode // (DEG * DEG), jnp.where(direction == 1, mode // DEG % DEG, mode % DEG))
    hit = (of_mode == degree) & (group < PER_VAR)
    return hit.astype(jnp.float32).astype(jnp.bfloat16)


def lower_modes():
    mode = iota((MODES, LANES), 0)
    most = jnp.maximum(jnp.maximum(mode // (DEG * DEG), mode // DEG % DEG), mode % DEG)
    return (most <= DEG - 2).astype(jnp.float32)


def fused_kernel(
    n_z, n_seat, n_rad, ta_hbm, tr_hbm, st_hbm, jac_hbm, lift_hbm, order_hbm, patch_hbm, out_ref, flag_ref,
    ta, tr, st, jac, lift_t, lift, order, patch, values, faces, acc, flat_r,
    rim_out, rim_in, ids_out, ids_in, place, choose, rows_out, rows_in, sums_out, sums_in,
    load_sem, state_sem, rim_sem, ids_sem, gather_sem, sum_sem,
):
    azi, rad = lax.axis_index("azi"), lax.axis_index("rad")
    n_azi = n_z * n_seat
    z, seat = azi // n_seat, azi % n_seat
    targets = n_seat * n_rad
    me = seat * n_rad + rad
    face_len, rows_azi, _ = ta.shape
    kmax = jac.shape[0]
    blocks = rows_azi // ROWS
    bands = rows_azi // BAND
    width = ROWS * LANES

    def towards(by_azi, by_rad):
        return {"azi": (azi + n_azi + by_azi) % n_azi, "rad": (rad + n_rad + by_rad) % n_rad}

    def at_z(peer):
        return {"azi": peer * n_seat + seat, "rad": rad}

    def at_target(peer):
        return {"azi": z * n_seat + peer // n_rad, "rad": peer % n_rad}

    barrier = pltpu.get_barrier_semaphore()
    senders = [towards(-1, 0), towards(0, -1)]
    senders += [at_z((z + k) % n_z) for k in range(1, n_z)]
    senders += [at_target((me + k) % targets) for k in range(1, targets)]
    for device in senders:
        pl.semaphore_signal(barrier, inc=1, device_id=device, device_id_type=MESH_ID)

    spans = []
    first_var = 0
    for part in PARTS:
        count = sum(len(pair) for pair in part)
        spans.append((first_var * MODES, count * MODES))
        first_var += count

    loads = [
        pltpu.make_async_copy(order_hbm, order, load_sem.at[0]),
        pltpu.make_async_copy(patch_hbm, patch, load_sem.at[1]),
        pltpu.make_async_copy(tr_hbm, tr, load_sem.at[2]),
        pltpu.make_async_copy(ta_hbm, ta, load_sem.at[3]),
        pltpu.make_async_copy(lift_hbm, lift_t, load_sem.at[4]),
    ]
    jac_loads = [
        pltpu.make_async_copy(jac_hbm.at[pl.ds(start, count)], jac.at[pl.ds(start, count)], load_sem.at[5 + i])
        for i, (start, count) in enumerate(spans)
    ]
    state_loads = [
        pltpu.make_async_copy(st_hbm.at[:, pl.ds(b * ROWS, ROWS), :], st.at[b], state_sem.at[b])
        for b in range(blocks)
    ]
    for copy in loads + [state_loads[0], jac_loads[0]]:
        copy.start()

    loads[2].wait()
    flat_r[...] = tr[...].reshape(face_len, rows_azi * LANES)
    lane = iota((face_len, LANES), 1)
    column = jnp.zeros((face_len, LANES), jnp.float32)
    for i in range(rows_azi):
        piece = flat_r[:, i * LANES : (i + 1) * LANES].astype(jnp.float32)
        column = jnp.where(lane == i, pltpu.roll(piece, (i + 1) % LANES, 1), column)
    rim_out[1] = column.astype(jnp.bfloat16)
    loads[3].wait()
    rim_out[0] = ta[:, rows_azi - 1, :]

    loads[0].wait()
    loads[1].wait()
    upto = (iota((LANES, LANES), 0) <= iota((LANES, LANES), 1)).astype(jnp.float32).astype(jnp.bfloat16)
    since = iota((LANES, LANES), 1) <= iota((LANES, LANES), 0)
    ones = jnp.ones((LANES, LANES), jnp.bfloat16)
    used = jnp.zeros((1, LANES), jnp.float32)
    ids = jnp.zeros((RUN_SLOTS, 1), jnp.float32)
    slot = iota((RUN_SLOTS, LANES), 0).astype(jnp.float32)
    slot_of = []
    for band in range(bands):
        row = patch[band * BAND : band * BAND + ROWS].astype(jnp.float32)
        start = jnp.where((iota(row.shape, 1) == 0) | (row != pltpu.roll(row, 1, 1)), 1.0, 0.0)
        rank_row = jnp.dot(start.astype(jnp.bfloat16), upto, preferred_element_type=jnp.float32)[:1] - 1.0 + used
        begun = jnp.where(since, start[:1], 0.0).astype(jnp.bfloat16)
        rank_col = jnp.dot(begun, ones, preferred_element_type=jnp.float32)
        mine = (slot == rank_row) & (start[:1] > 0.0)
        ids = ids + jnp.sum(jnp.where(mine, row[:1] + 1.0, 0.0), axis=1, keepdims=True)
        slot_of.append(rank_col - 1.0 + used)
        used = used + rank_col[LANES - 1 :]
    differ = jnp.zeros((1, 1), jnp.float32)
    for band in range(bands):
        rows = patch[band * BAND : (band + 1) * BAND]
        uneven = jnp.max((rows != rows[:1]).astype(jnp.float32), axis=0, keepdims=True)
        differ = jnp.maximum(differ, jnp.max(uneven, axis=1, keepdims=True))
    slot_id = jnp.broadcast_to(ids - 1.0, ids_out.shape)
    ids_out[...] = jnp.where(slot == float(FLAG_SLOT), -1.0 - differ, slot_id)
    ids_in[z] = ids_out[...]

    slot_lane = iota((LANES, LANES), 1).astype(jnp.float32)
    for side in range(2):
        for band in range(bands):
            begin = (side * bands + band) * LANES
            hit = slot_of[band] == slot_lane - float(side * RUN_SLOTS)
            place[begin : begin + LANES] = hit.astype(jnp.float32).astype(jnp.bfloat16)

    def rim_copy(which, target):
        return pltpu.make_async_remote_copy(
            src_ref=rim_out.at[which], dst_ref=rim_in.at[which],
            send_sem=rim_sem.at[0, which], recv_sem=rim_sem.at[1, which],
            device_id=target, device_id_type=MESH_ID,
        )

    def ids_copy(peer, source):
        return pltpu.make_async_remote_copy(
            src_ref=ids_out, dst_ref=ids_in.at[source],
            send_sem=ids_sem.at[0, peer], recv_sem=ids_sem.at[1, source],
            device_id=at_z(peer), device_id_type=MESH_ID,
        )

    def gather_copy(part, peer, source):
        span = pl.ds(pair_start[part], len(PARTS[part]))
        return pltpu.make_async_remote_copy(
            src_ref=rows_out.at[span], dst_ref=rows_in.at[source, span],
            send_sem=gather_sem.at[0, part, peer], recv_sem=gather_sem.at[1, part, source],
            device_id=at_z(peer), device_id_type=MESH_ID,
        )

    def sum_copy(part, peer, source):
        span = pl.ds(pair_start[part], len(PARTS[part]))
        return pltpu.make_async_remote_copy(
            src_ref=sums_out.at[peer, span], dst_ref=sums_in.at[source, span],
            send_sem=sum_sem.at[0, part, peer], recv_sem=sum_sem.at[1, part, source],
            device_id=at_target(peer), device_id_type=MESH_ID,
        )

    pair_start = [sum(len(part) for part in PARTS[:i]) for i in range(len(PARTS))]
    z_peers = [((z + k) % n_z, (z + n_z - k) % n_z) for k in range(1, n_z)]
    plane_peers = [((me + k) % targets, (me + targets - k) % targets) for k in range(1, targets)]

    pl.semaphore_wait(barrier, len(senders))
    rims = [rim_copy(0, towards(1, 0)), rim_copy(1, towards(0, 1))]
    for copy in rims:
        copy.start()
    for peer, source in z_peers:
        ids_copy(peer, z).start()

    loads[4].wait()
    lift[...] = lift_t[...].T
    lower = lower_modes()
    table = group_table()
    lower_all = jnp.concatenate([lower] * VARS, axis=0)
    lower_all_16 = lower_all.astype(jnp.bfloat16)

    def flag_row(row):
        return (order[row : row + 1] == DEG - 1).astype(jnp.float32)

    def stage_values(b):
        keep = jnp.concatenate(
            [jnp.maximum(lower_all_16, flag_row(b * ROWS + i).astype(jnp.bfloat16)) for i in range(ROWS)], axis=1
        )
        values[b] = st[b].reshape(kmax, width) * keep

    def stage_faces(b):
        ta_b = ta[:, b * ROWS : (b + 1) * ROWS, :].reshape(face_len, width)
        if b == 0:
            before = rim_in[0]
        else:
            before = ta[:, b * ROWS - 1, :]
        tr_b = flat_r[:, b * width : (b + 1) * width]
        rim = rim_in[1].astype(jnp.float32)
        pieces = []
        for i in range(ROWS):
            moved = pltpu.roll(tr_b[:, i * LANES : (i + 1) * LANES].astype(jnp.float32), 1, 1)
            row = b * ROWS + i
            edge = pltpu.roll(rim, (LANES - row) % LANES, 1)
            pieces.append(jnp.where(lane == 0, jnp.where(rad > 0, edge, 0.0), moved).astype(jnp.bfloat16))
        faces[b, 0:face_len] = ta_b
        faces[b, face_len : 2 * face_len] = jnp.concatenate([before, ta_b[:, : width - LANES]], axis=1)
        faces[b, 2 * face_len : 3 * face_len] = tr_b
        faces[b, 3 * face_len :] = jnp.concatenate(pieces, axis=1)

    def weigh(part, b, residual):
        start, count = spans[part]
        adjoint = jnp.dot(lift[start : start + count], faces[b], preferred_element_type=jnp.float32)
        low = lower_all[start : start + count]
        total = None
        for i in range(ROWS):
            cut = slice(i * LANES, (i + 1) * LANES)
            term = adjoint[:, cut] * residual[:, cut] * jnp.maximum(low, flag_row(b * ROWS + i))
            total = term if total is None else total + term
        return total

    def residual_of(part, b):
        start, count = spans[part]
        return jnp.dot(jac[start : start + count], values[b], preferred_element_type=jnp.float32)

    def add_block(part, b, total):
        start, count = spans[part]
        band = b * ROWS // BAND
        if b * ROWS % BAND == 0:
            acc[band, start : start + count] = total
        else:
            acc[band, start : start + count] += total

    def send_rows(part):
        halves_of = []
        for var in [var for pair in PARTS[part] for var in pair]:
            for band in range(bands):
                halves_of += float_halves(acc[band, var * MODES : (var + 1) * MODES])
        both = jnp.concatenate(halves_of, axis=1).astype(jnp.bfloat16)
        sums = jnp.dot(table, both, preferred_element_type=jnp.float32)
        begin = 0
        for p, pair in enumerate(PARTS[part], pair_start[part]):
            terms = []
            for i in range(len(pair) * bands):
                at = begin + 2 * i * LANES
                terms.append(sums[:, at : at + LANES] + sums[:, at + LANES : at + 2 * LANES])
            begin += 2 * len(terms) * LANES
            rows_out[p] = table_dot(jnp.concatenate(terms, axis=1), place[: len(terms) * LANES])
        for peer, source in z_peers:
            gather_copy(part, peer, z).start()
        span = pl.ds(pair_start[part], len(PARTS[part]))
        rows_in[z, span] = rows_out[span]

    def send_sums(part):
        for peer, source in z_peers:
            gather_copy(part, peer, source).wait_recv()
        flags = [ids_in[peer, FLAG_SLOT : FLAG_SLOT + 1] for peer in range(n_z)]
        flag = -1.0 - functools.reduce(jnp.minimum, flags)
        held = range(pair_start[part], pair_start[part] + len(PARTS[part]))
        terms = [jnp.concatenate([rows_in[peer, p] for peer in range(n_z)], axis=1) for p in held]
        sums = table_dot(jnp.concatenate(terms, axis=0), choose[...])
        for i, p in enumerate(held):
            for target in range(targets):
                piece = sums[i * GROUP_ROWS : (i + 1) * GROUP_ROWS, target * LANES : (target + 1) * LANES]
                if p == 0:
                    piece = jnp.where(iota(piece.shape, 0) == GROUP_ROWS - 1, flag, piece)
                sums_out[target, p] = piece
        for peer, source in plane_peers:
            sum_copy(part, peer, me).start()
        span = pl.ds(pair_start[part], len(PARTS[part]))
        sums_in[me, span] = sums_out[me, span]

    def make_choose():
        for peer, source in z_peers:
            ids_copy(peer, source).wait_recv()
        here = iota((1, LANES), 1)
        sides = []
        for side in range(2):
            inside = (here >= side * PATCH_DEV) & (here < (side + 1) * PATCH_DEV)
            sides.append(jnp.where(inside, here - side * PATCH_DEV, -(2**20)).astype(jnp.float32))
        base = (z * targets * PATCH_DEV).astype(jnp.float32)
        for peer in range(n_z):
            for side in range(2):
                begin = (2 * peer + side) * RUN_SLOTS
                for target in range(targets):
                    hit = ids_in[peer] == sides[side] + (base + float(target * PATCH_DEV))
                    choose[begin : begin + RUN_SLOTS, target * LANES : (target + 1) * LANES] = hit.astype(
                        jnp.float32
                    ).astype(jnp.bfloat16)

    state_loads[0].wait()
    for copy in state_loads[1:] + jac_loads[1:]:
        copy.start()
    stage_values(0)
    jac_loads[0].wait()
    first = residual_of(0, 0)
    state_loads[1].wait()
    stage_values(1)
    second = residual_of(0, 1)
    for copy in rims:
        copy.wait_recv()
    for b in range(blocks):
        if b > 1:
            state_loads[b].wait()
            stage_values(b)
        stage_faces(b)
        residual = (first, second)[b] if b < 2 else residual_of(0, b)
        add_block(0, b, weigh(0, b, residual))
    send_rows(0)
    jac_loads[1].wait()
    for b in range(blocks):
        add_block(1, b, weigh(1, b, residual_of(1, b)))
        if b == 0:
            make_choose()
        if b == min(1, blocks - 1):
            send_sums(0)
    send_rows(1)
    send_sums(1)
    columns = []
    for part, pairs in enumerate(PARTS):
        for peer, source in plane_peers:
            sum_copy(part, peer, source).wait_recv()
        span = slice(pair_start[part], pair_start[part] + len(pairs))
        total = functools.reduce(jnp.add, [sums_in[source, span] for source in range(targets)])
        total = jnp.abs(total).reshape(len(pairs) * GROUP_ROWS, LANES)
        if part == 0:
            flag_ref[0, 0] = jnp.where(jnp.max(total[GROUP_ROWS - 1 : GROUP_ROWS]) > 0.0, 1, 0)
        pad = jnp.zeros((LANES - len(pairs) * GROUP_ROWS, LANES), jnp.float32)
        turned = jnp.concatenate([total, pad], axis=0).T
        for p, pair in enumerate(pairs):
            for side in range(len(pair)):
                columns.append(
                    turned[side * PATCH_DEV : (side + 1) * PATCH_DEV, p * GROUP_ROWS : p * GROUP_ROWS + PER_VAR]
                )
    out_ref[...] = jnp.concatenate(columns, axis=1)

    for copy in rims:
        copy.wait_send()
    for peer, source in z_peers:
        ids_copy(peer, z).wait_send()
    for part in range(len(PARTS)):
        for peer, source in z_peers:
            gather_copy(part, peer, z).wait_send()
        for peer, source in plane_peers:
            sum_copy(part, peer, me).wait_send()


def per_device(trace_azimuth, trace_radial, state, jacobian, lift_map, order, patch):
    face_len, rows_azi, rows_rad = trace_azimuth.shape
    kmax = jacobian.shape[0]
    n_azi, n_rad = lax.axis_size("azi"), lax.axis_size("rad")
    n_seat = SEATS if n_azi % SEATS == 0 else 1
    n_z, targets = n_azi // n_seat, n_seat * n_rad
    blocks = rows_azi // ROWS
    width = ROWS * LANES
    pairs = sum(len(part) for part in PARTS)
    f32, b16 = jnp.float32, jnp.bfloat16
    out, uneven = pl.pallas_call(
        functools.partial(fused_kernel, n_z, n_seat, n_rad),
        out_shape=(jax.ShapeDtypeStruct((PATCH_DEV, GROUPS), f32), jax.ShapeDtypeStruct((1, 1), jnp.int32)),
        in_specs=[pl.BlockSpec(memory_space=pl.ANY)] * 7,
        out_specs=(pl.BlockSpec(memory_space=pltpu.VMEM), pl.BlockSpec(memory_space=pltpu.SMEM)),
        scratch_shapes=[
            pltpu.VMEM(trace_azimuth.shape, b16),
            pltpu.VMEM(trace_radial.shape, b16),
            pltpu.VMEM((blocks, kmax, ROWS, LANES), b16),
            pltpu.VMEM(jacobian.shape, b16),
            pltpu.VMEM(lift_map.shape[::-1], b16),
            pltpu.VMEM(lift_map.shape, b16),
            pltpu.VMEM(order.shape, jnp.int32),
            pltpu.VMEM(patch.shape, jnp.int32),
            pltpu.VMEM((blocks, kmax, width), b16),
            pltpu.VMEM((blocks, 4 * face_len, width), b16),
            pltpu.VMEM((rows_azi // BAND, kmax, LANES), f32),
            pltpu.VMEM((face_len, rows_azi * LANES), b16),
            pltpu.VMEM((2, face_len, LANES), b16),
            pltpu.VMEM((2, face_len, LANES), b16),
            pltpu.VMEM((RUN_SLOTS, LANES), f32),
            pltpu.VMEM((n_z, RUN_SLOTS, LANES), f32),
            pltpu.VMEM((rows_azi // BAND * 2 * LANES, LANES), b16),
            pltpu.VMEM((n_z * 2 * RUN_SLOTS, targets * LANES), b16),
            pltpu.VMEM((pairs, GROUP_ROWS, LANES), f32),
            pltpu.VMEM((n_z, pairs, GROUP_ROWS, LANES), f32),
            pltpu.VMEM((targets, pairs, GROUP_ROWS, LANES), f32),
            pltpu.VMEM((targets, pairs, GROUP_ROWS, LANES), f32),
            pltpu.SemaphoreType.DMA((5 + len(PARTS),)),
            pltpu.SemaphoreType.DMA((blocks,)),
            pltpu.SemaphoreType.DMA((2, 2)),
            pltpu.SemaphoreType.DMA((2, n_z)),
            pltpu.SemaphoreType.DMA((2, len(PARTS), n_z)),
            pltpu.SemaphoreType.DMA((2, len(PARTS), targets)),
        ],
        compiler_params=pltpu.CompilerParams(collective_id=0, has_side_effects=True, vmem_limit_bytes=VLIM),
        cost_estimate=pl.CostEstimate(
            flops=2 * kmax * (kmax + 4 * face_len) * rows_azi * rows_rad,
            bytes_accessed=2 * kmax * rows_azi * rows_rad, transcendentals=0,
        ),
    )(trace_azimuth, trace_radial, state, jacobian, lift_map.T, order, patch)
    arguments = (trace_azimuth, trace_radial, state, jacobian, lift_map, order, patch)
    return lax.cond(uneven[0, 0] != 0, general_path, lambda *unused: out, *arguments)


def solution(mesh):
    in_specs = (
        P(None, "azi", "rad"),
        P(None, "azi", "rad"),
        P(None, "azi", "rad"),
        P(),
        P(),
        P("azi", "rad"),
        P("azi", "rad"),
    )
    out_specs = P(("azi", "rad"), None)
    return jax.shard_map(
        per_device, mesh=mesh, in_specs=in_specs, out_specs=out_specs, check_vma=False
    )
```

```python
import functools

import jax
import jax.numpy as jnp
import numpy as np
from jax import lax
from jax.experimental import pallas as pl
from jax.experimental.pallas import tpu as pltpu
from jax.sharding import PartitionSpec as P

DEG = 6
MODES = 216
KMAX = 1080
GROUPS = 90
PATCH_DEV = 48
BAND = 16
ROWS = 8
LANES = 128
SLOTS = 56
ID_LANE = LANES - 1
SUBS = 1
VLIM_RIM = 57 * 1024 * 1024
VLIM_MAIN = 57 * 1024 * 1024
SEATS = 2
DIRS = 3
VARS = 5
PER_VAR = DIRS * DEG
GROUP_ROWS = 24
RUN_SLOTS = 64
FLAG_SLOT = RUN_SLOTS - 1
DEPTH = 256
VLIM = 57 * 1024 * 1024
PARTS = (((0, 1), (2,)), ((3, 4),))
MESH_ID = pl.DeviceIdType.MESH


def rim_kernel(n_azi, n_rad, ta_ref, tr_ref, rim_a_ref, rim_r_ref, outgoing, recv, send_sem, recv_sem):
    azi, rad = lax.axis_index("azi"), lax.axis_index("rad")
    mesh_id = pl.DeviceIdType.MESH
    barrier = pltpu.get_barrier_semaphore()

    def towards(by_azi, by_rad):
        return {"azi": (azi + n_azi + by_azi) % n_azi, "rad": (rad + n_rad + by_rad) % n_rad}

    pl.semaphore_signal(barrier, inc=1, device_id=towards(-1, 0), device_id_type=mesh_id)
    pl.semaphore_signal(barrier, inc=1, device_id=towards(0, -1), device_id_type=mesh_id)

    outgoing[0] = ta_ref[:, ta_ref.shape[1] - 1, :]
    face_len, rows_azi, lanes = tr_ref.shape
    flat = tr_ref[...].reshape(face_len, rows_azi * lanes)
    lane = lax.broadcasted_iota(jnp.int32, (face_len, lanes), 1)
    column = jnp.zeros((face_len, lanes), jnp.float32)
    for i in range(rows_azi):
        piece = flat[:, i * lanes : (i + 1) * lanes].astype(jnp.float32)
        column = jnp.where(lane == i, pltpu.roll(piece, (i + 1) % lanes, 1), column)
    outgoing[1] = column.astype(jnp.bfloat16)

    pl.semaphore_wait(barrier, 2)
    copies = []
    for slot, target in enumerate((towards(1, 0), towards(0, 1))):
        copies.append(
            pltpu.make_async_remote_copy(
                src_ref=outgoing.at[slot], dst_ref=recv.at[slot],
                send_sem=send_sem.at[slot], recv_sem=recv_sem.at[slot],
                device_id=target, device_id_type=mesh_id,
            )
        )
    for copy in copies:
        copy.start()
    for copy in copies:
        copy.wait()
    rim_a_ref[...] = recv[0]
    rim_r_ref[...] = jnp.where(rad > 0, recv[1], jnp.zeros_like(recv[1]))


def mode_tables():
    mode_index = np.arange(KMAX)
    variable = mode_index // MODES
    inside = mode_index % MODES
    degrees = [inside // (DEG * DEG), inside // DEG % DEG, inside % DEG]
    lower_modes = np.maximum(np.maximum(degrees[0], degrees[1]), degrees[2]) <= DEG - 2
    group_index = np.arange(LANES)
    group_table = np.zeros((LANES, KMAX), np.float32)
    for direction in range(3):
        target = variable * 3 * DEG + direction * DEG + degrees[direction]
        group_table = group_table + (group_index[:, None] == target[None, :]).astype(np.float32)
    return (lower_modes, group_table)


def halves(value):
    high = value.astype(jnp.bfloat16)
    low = (value - high.astype(jnp.float32)).astype(jnp.bfloat16)
    return high, low


def exact_table_dot(table, value):
    high, low = halves(value)
    dims = (((1,), (1,)), ((), ()))
    return lax.dot_general(table, high, dims, preferred_element_type=jnp.float32) + lax.dot_general(
        table, low, dims, preferred_element_type=jnp.float32
    )


def slot_ids_of_runs(patch, rows_azi):
    slot = lax.broadcasted_iota(jnp.int32, (SLOTS, LANES), 0).astype(jnp.float32)
    upto = lax.broadcasted_iota(jnp.int32, (LANES, LANES), 0) <= lax.broadcasted_iota(
        jnp.int32, (LANES, LANES), 1
    )
    used = jnp.zeros((1, 1), jnp.float32)
    ids = jnp.zeros((SLOTS, 1), jnp.float32)
    for band in range(0, rows_azi, BAND):
        row = patch[band : band + 8].astype(jnp.float32)
        lane = lax.broadcasted_iota(jnp.int32, row.shape, 1)
        start = jnp.where((lane == 0) | (row != pltpu.roll(row, 1, 1)), 1.0, 0.0)
        rank = jnp.dot(
            start.astype(jnp.bfloat16), upto.astype(jnp.bfloat16), preferred_element_type=jnp.float32
        )
        mine = (slot == rank[:1] - 1.0 + used) & (start[:1] > 0.0)
        ids = ids + jnp.sum(jnp.where(mine, row[:1] + 1.0, 0.0), axis=1, keepdims=True)
        used = used + jnp.sum(start[:1], axis=1, keepdims=True)
    return ids.astype(jnp.int32) - 1


def local_kernel(
    ta_ref, tr_ref, st_ref, jac_ref, lift_ref, order_ref, patch_ref, lower_ref, table_ref,
    rim_a_ref, rim_r_ref, out_ref, carry, acc, lift, slots, jac, jac_sem,
):
    step = pl.program_id(0)
    fetch = pltpu.make_async_copy(jac_ref, jac, jac_sem)

    @pl.when(step == 0)
    def _():
        fetch.start()

    width = ROWS * LANES
    rows_azi = patch_ref.shape[0]
    face_len = ta_ref.shape[0]
    steps_band = BAND // ROWS

    all_patch = patch_ref[...]
    differ = jnp.int32(0)
    for band in range(0, rows_azi, BAND):
        rows = all_patch[band : band + BAND]
        differ = jnp.maximum(differ, jnp.max((rows != rows[:1]).astype(jnp.int32)))

    @pl.when(step == 0)
    def _():
        carry[...] = rim_a_ref[...]
        out_ref[...] = jnp.zeros_like(out_ref)
        lift[...] = lift_ref[...].T
        slots[...] = jnp.broadcast_to(slot_ids_of_runs(all_patch, rows_azi), slots.shape)

    @pl.when((step == 0) & (differ != 0))
    def _():
        none = jnp.int32(2**30)
        where_slot = lax.broadcasted_iota(jnp.int32, slots.shape, 0)

        def next_id(slot, last):
            found = jnp.min(jnp.where(all_patch > last, all_patch, none))
            slots[...] = jnp.where(where_slot == slot, jnp.where(found == none, -1, found), slots[...])
            return found

        lax.fori_loop(0, SLOTS, next_id, jnp.int32(-1))

    ta = ta_ref[...].reshape(face_len, width)
    tr = tr_ref[...].reshape(face_len, width)
    behind_a = jnp.concatenate([carry[...], ta[:, : width - LANES]], axis=1)
    carry[...] = ta[:, width - LANES :]
    row_id = lax.broadcasted_iota(jnp.int32, (rows_azi, width), 0)
    lane_id = lax.broadcasted_iota(jnp.int32, (rows_azi, width), 1)
    spread = ((row_id - step * ROWS) * LANES == lane_id).astype(jnp.bfloat16)
    rim = jnp.dot(rim_r_ref[:, :rows_azi], spread, preferred_element_type=jnp.float32)
    moved = pltpu.roll(tr.astype(jnp.float32), 1, 1)
    first = lax.broadcasted_iota(jnp.int32, (face_len, width), 1) % LANES == 0
    behind_r = jnp.where(first, rim, moved).astype(jnp.bfloat16)
    faces = jnp.concatenate([ta, behind_a, tr, behind_r], axis=0)

    @pl.when(step == 0)
    def _():
        fetch.wait()

    flags = (order_ref[...] == DEG - 1).astype(jnp.float32)
    sub = ROWS // SUBS

    def product_rows(index):
        span = slice(index * sub, (index + 1) * sub)
        cut = slice(index * sub * LANES, (index + 1) * sub * LANES)
        keep = jnp.maximum(lower_ref[...], flags[span].reshape(1, sub * LANES))
        values = st_ref[:, span, :].reshape(KMAX, sub * LANES) * keep.astype(jnp.bfloat16)
        adjoint = jnp.dot(lift[...], faces[:, cut], preferred_element_type=jnp.float32)
        residual = jnp.dot(jac[...], values, preferred_element_type=jnp.float32)
        product = adjoint * residual * keep
        return [product[:, row * LANES : (row + 1) * LANES] for row in range(sub)]

    band_start = pl.multiple_of(step // steps_band * BAND, BAND)
    band_row = patch_ref[pl.ds(band_start, 1), :]
    mine = patch_ref[pl.ds(pl.multiple_of(step * ROWS, ROWS), ROWS), :]
    place = slots[...]

    def add_to_patches(columns, row):
        grouped = exact_grouped(columns)
        chosen = (place == row).astype(jnp.bfloat16)
        out_ref[...] += exact_table_dot(chosen, grouped)

    def exact_grouped(columns):
        both = jnp.concatenate(halves(columns), axis=1)
        sums = jnp.dot(table_ref[...], both, preferred_element_type=jnp.float32)
        return sums[:, :LANES] + sums[:, LANES:]

    @pl.when(step % steps_band == 0)
    def _():
        acc[...] = jnp.zeros_like(acc)

    @pl.when(differ == 0)
    def _():
        for index in range(SUBS):
            acc[...] += functools.reduce(jnp.add, product_rows(index))

    @pl.when(differ != 0)
    def _():
        for index in range(SUBS):
            for row, product in enumerate(product_rows(index), index * sub):
                add_to_patches(product, mine[row : row + 1])

    @pl.when(step % steps_band == steps_band - 1)
    def _():
        @pl.when(differ == 0)
        def _():
            add_to_patches(acc[...], band_row)

    @pl.when(step == pl.num_programs(0) - 1)
    def _():
        lane = lax.broadcasted_iota(jnp.int32, out_ref.shape, 1)
        out_ref[...] = jnp.where(lane == ID_LANE, place.astype(jnp.float32), out_ref[...])


def exchange_kernel(
    n_z, n_seat, n_rad, rows_ref, out_ref, gathered, outgoing, recv,
    gather_send, gather_recv, sum_send, sum_recv,
):
    azi, rad = lax.axis_index("azi"), lax.axis_index("rad")
    z, seat = azi // n_seat, azi % n_seat
    targets = n_seat * n_rad
    me = seat * n_rad + rad
    mesh_id = pl.DeviceIdType.MESH

    def at_z(peer):
        return {"azi": peer * n_seat + seat, "rad": rad}

    def at_target(peer):
        return {"azi": z * n_seat + peer // n_rad, "rad": peer % n_rad}

    barrier = pltpu.get_barrier_semaphore()
    for k in range(1, n_z):
        pl.semaphore_signal(barrier, inc=1, device_id=at_z((z + k) % n_z), device_id_type=mesh_id)
    for k in range(1, targets):
        pl.semaphore_signal(
            barrier, inc=1, device_id=at_target((me + k) % targets), device_id_type=mesh_id
        )
    pl.semaphore_wait(barrier, n_z + targets - 2)

    def gather_copy(peer, source):
        return pltpu.make_async_remote_copy(
            src_ref=rows_ref, dst_ref=gathered.at[source],
            send_sem=gather_send.at[peer], recv_sem=gather_recv.at[source],
            device_id=at_z(peer), device_id_type=mesh_id,
        )

    def sum_copy(peer, source):
        return pltpu.make_async_remote_copy(
            src_ref=outgoing.at[peer], dst_ref=recv.at[source],
            send_sem=sum_send.at[peer], recv_sem=sum_recv.at[source],
            device_id=at_target(peer), device_id_type=mesh_id,
        )

    for k in range(1, n_z):
        gather_copy((z + k) % n_z, z).start()
    gathered[z] = rows_ref[...]
    for k in range(1, n_z):
        gather_copy((z + k) % n_z, (z + n_z - k) % n_z).wait_recv()

    rows = gathered[...].reshape(n_z * SLOTS, LANES)
    pick = (lax.broadcasted_iota(jnp.int32, (8, LANES), 1) == ID_LANE).astype(jnp.bfloat16)
    ids = exact_table_dot(pick, rows)[:1]
    count = targets * PATCH_DEV
    wanted = (z * count + lax.broadcasted_iota(jnp.int32, (count, n_z * SLOTS), 0)).astype(jnp.float32)
    chosen = (wanted == ids).astype(jnp.bfloat16)
    both = jnp.dot(
        chosen, jnp.concatenate(halves(rows), axis=1), preferred_element_type=jnp.float32
    )
    outgoing[...] = (both[:, :LANES] + both[:, LANES:]).reshape(targets, PATCH_DEV, LANES)

    for k in range(1, targets):
        sum_copy((me + k) % targets, me).start()
    total = outgoing[me]
    for k in range(1, targets):
        source = (me + targets - k) % targets
        sum_copy((me + k) % targets, source).wait_recv()
        total = total + recv[source]
    for k in range(1, n_z):
        gather_copy((z + k) % n_z, z).wait_send()
    for k in range(1, targets):
        sum_copy((me + k) % targets, me).wait_send()
    out_ref[...] = jnp.abs(total)[:, : out_ref.shape[1]]


def general_path(trace_azimuth, trace_radial, state, jacobian, lift_map, order, patch):
    face_len, rows_azi, rows_rad = trace_azimuth.shape
    n_azi, n_rad = lax.axis_size("azi"), lax.axis_size("rad")
    n_seat = SEATS if n_azi % SEATS == 0 else 1
    n_z, targets = n_azi // n_seat, n_seat * n_rad
    rim = jax.ShapeDtypeStruct((face_len, LANES), jnp.bfloat16)
    rim_azimuth, rim_radial = pl.pallas_call(
        functools.partial(rim_kernel, n_azi, n_rad),
        grid=(1,),
        out_shape=(rim, rim),
        in_specs=[
            pl.BlockSpec((face_len, ROWS, LANES), lambda t: (0, rows_azi // ROWS - 1, 0)),
            pl.BlockSpec(trace_radial.shape, lambda t: (0, 0, 0)),
        ],
        out_specs=(pl.BlockSpec(rim.shape, lambda t: (0, 0)),) * 2,
        scratch_shapes=[
            pltpu.VMEM((2,) + rim.shape, jnp.bfloat16),
            pltpu.VMEM((2,) + rim.shape, jnp.bfloat16),
            pltpu.SemaphoreType.DMA((2,)),
            pltpu.SemaphoreType.DMA((2,)),
        ],
        compiler_params=pltpu.CompilerParams(
            collective_id=2, has_side_effects=True, vmem_limit_bytes=VLIM_RIM
        ),
        cost_estimate=pl.CostEstimate(flops=0, bytes_accessed=12_000_000, transcendentals=0),
    )(trace_azimuth, trace_radial)
    lower_np, group_np = mode_tables()
    lower = jnp.asarray(lower_np.astype(np.float32)[:, None])
    table = jnp.asarray(group_np, jnp.bfloat16)

    def whole(shape):
        return pl.BlockSpec(shape, lambda t: (0,) * len(shape))

    def part(depth):
        return pl.BlockSpec((depth, ROWS, LANES), lambda t: (0, t, 0))

    rows = pl.pallas_call(
        local_kernel,
        grid=(rows_azi // ROWS,),
        out_shape=jax.ShapeDtypeStruct((SLOTS, LANES), jnp.float32),
        in_specs=[
            part(face_len), part(face_len), part(KMAX),
            pl.BlockSpec(memory_space=pl.ANY), whole(lift_map.shape[::-1]),
            pl.BlockSpec((ROWS, LANES), lambda t: (t, 0)), whole(patch.shape),
            whole(lower.shape), whole(table.shape),
            whole(rim_azimuth.shape), whole(rim_radial.shape),
        ],
        out_specs=whole((SLOTS, LANES)),
        scratch_shapes=[
            pltpu.VMEM((face_len, LANES), jnp.bfloat16),
            pltpu.VMEM((KMAX, LANES), jnp.float32),
            pltpu.VMEM(lift_map.shape, jnp.bfloat16),
            pltpu.VMEM((SLOTS, LANES), jnp.int32),
            pltpu.VMEM(jacobian.shape, jnp.bfloat16),
            pltpu.SemaphoreType.DMA,
        ],
        compiler_params=pltpu.CompilerParams(
            dimension_semantics=("arbitrary",), vmem_limit_bytes=VLIM_MAIN
        ),
        cost_estimate=pl.CostEstimate(
            flops=2 * KMAX * (KMAX + 4 * face_len) * rows_azi * rows_rad,
            bytes_accessed=2 * KMAX * rows_azi * rows_rad, transcendentals=0,
        ),
    )(trace_azimuth, trace_radial, state, jacobian, lift_map.T, order, patch, lower, table,
      rim_azimuth, rim_radial)

    return pl.pallas_call(
        functools.partial(exchange_kernel, n_z, n_seat, n_rad),
        out_shape=jax.ShapeDtypeStruct((PATCH_DEV, GROUPS), jnp.float32),
        in_specs=[pl.BlockSpec(memory_space=pltpu.VMEM)],
        out_specs=pl.BlockSpec(memory_space=pltpu.VMEM),
        scratch_shapes=[
            pltpu.VMEM((n_z, SLOTS, LANES), jnp.float32),
            pltpu.VMEM((targets, PATCH_DEV, LANES), jnp.float32),
            pltpu.VMEM((targets, PATCH_DEV, LANES), jnp.float32),
            pltpu.SemaphoreType.DMA((n_z,)),
            pltpu.SemaphoreType.DMA((n_z,)),
            pltpu.SemaphoreType.DMA((targets,)),
            pltpu.SemaphoreType.DMA((targets,)),
        ],
        compiler_params=pltpu.CompilerParams(collective_id=1, has_side_effects=True),
    )(rows)


def iota(shape, dim):
    return lax.broadcasted_iota(jnp.int32, shape, dim)


def float_halves(value):
    high = value.astype(jnp.bfloat16).astype(jnp.float32)
    return high, value - high


def table_dot(value, table):
    rows = value.shape[0]
    both = jnp.concatenate(float_halves(value), axis=0).astype(jnp.bfloat16)
    sums = jnp.dot(both, table, preferred_element_type=jnp.float32)
    return sums[:rows] + sums[rows:]


def group_table():
    group = iota((GROUP_ROWS, MODES), 0)
    mode = iota((GROUP_ROWS, MODES), 1)
    direction, degree = group // DEG, group % DEG
    of_mode = jnp.where(direction == 0, mode // (DEG * DEG), jnp.where(direction == 1, mode // DEG % DEG, mode % DEG))
    hit = (of_mode == degree) & (group < PER_VAR)
    return hit.astype(jnp.float32).astype(jnp.bfloat16)


def lower_modes():
    mode = iota((MODES, LANES), 0)
    most = jnp.maximum(jnp.maximum(mode // (DEG * DEG), mode // DEG % DEG), mode % DEG)
    return (most <= DEG - 2).astype(jnp.float32)


def fused_kernel(
    n_z, n_seat, n_rad, ta_hbm, tr_hbm, st_hbm, jac_hbm, lift_hbm, order_hbm, patch_hbm, out_ref, flag_ref,
    ta, tr, st, jac, lift_t, lift, order, patch, values, faces, acc, flat_r,
    rim_out, rim_in, ids_out, ids_in, place, choose, rows_out, rows_in, sums_out, sums_in,
    load_sem, state_sem, rim_sem, ids_sem, gather_sem, sum_sem,
):
    azi, rad = lax.axis_index("azi"), lax.axis_index("rad")
    n_azi = n_z * n_seat
    z, seat = azi // n_seat, azi % n_seat
    targets = n_seat * n_rad
    me = seat * n_rad + rad
    face_len, rows_azi, _ = ta.shape
    kmax = jac.shape[0]
    blocks = rows_azi // ROWS
    bands = rows_azi // BAND
    width = ROWS * LANES

    def towards(by_azi, by_rad):
        return {"azi": (azi + n_azi + by_azi) % n_azi, "rad": (rad + n_rad + by_rad) % n_rad}

    def at_z(peer):
        return {"azi": peer * n_seat + seat, "rad": rad}

    def at_target(peer):
        return {"azi": z * n_seat + peer // n_rad, "rad": peer % n_rad}

    barrier = pltpu.get_barrier_semaphore()
    senders = [towards(-1, 0), towards(0, -1)]
    senders += [at_z((z + k) % n_z) for k in range(1, n_z)]
    senders += [at_target((me + k) % targets) for k in range(1, targets)]
    for device in senders:
        pl.semaphore_signal(barrier, inc=1, device_id=device, device_id_type=MESH_ID)

    spans = []
    first_var = 0
    for part in PARTS:
        count = sum(len(pair) for pair in part)
        spans.append((first_var * MODES, count * MODES))
        first_var += count

    loads = [
        pltpu.make_async_copy(order_hbm, order, load_sem.at[0]),
        pltpu.make_async_copy(patch_hbm, patch, load_sem.at[1]),
        pltpu.make_async_copy(tr_hbm, tr, load_sem.at[2]),
        pltpu.make_async_copy(ta_hbm, ta, load_sem.at[3]),
        pltpu.make_async_copy(lift_hbm, lift_t, load_sem.at[4]),
    ]
    jac_loads = [
        pltpu.make_async_copy(jac_hbm.at[pl.ds(start, count)], jac.at[pl.ds(start, count)], load_sem.at[5 + i])
        for i, (start, count) in enumerate(spans)
    ]
    state_loads = [
        pltpu.make_async_copy(st_hbm.at[:, pl.ds(b * ROWS, ROWS), :], st.at[b], state_sem.at[b])
        for b in range(blocks)
    ]
    for copy in loads + [state_loads[0], jac_loads[0]]:
        copy.start()

    loads[2].wait()
    flat_r[...] = tr[...].reshape(face_len, rows_azi * LANES)
    lane = iota((face_len, LANES), 1)
    column = jnp.zeros((face_len, LANES), jnp.float32)
    for i in range(rows_azi):
        piece = flat_r[:, i * LANES : (i + 1) * LANES].astype(jnp.float32)
        column = jnp.where(lane == i, pltpu.roll(piece, (i + 1) % LANES, 1), column)
    rim_out[1] = column.astype(jnp.bfloat16)
    loads[3].wait()
    rim_out[0] = ta[:, rows_azi - 1, :]

    loads[0].wait()
    loads[1].wait()
    upto = (iota((LANES, LANES), 0) <= iota((LANES, LANES), 1)).astype(jnp.float32).astype(jnp.bfloat16)
    since = iota((LANES, LANES), 1) <= iota((LANES, LANES), 0)
    ones = jnp.ones((LANES, LANES), jnp.bfloat16)
    used = jnp.zeros((1, LANES), jnp.float32)
    ids = jnp.zeros((RUN_SLOTS, 1), jnp.float32)
    slot = iota((RUN_SLOTS, LANES), 0).astype(jnp.float32)
    slot_of = []
    for band in range(bands):
        row = patch[band * BAND : band * BAND + ROWS].astype(jnp.float32)
        start = jnp.where((iota(row.shape, 1) == 0) | (row != pltpu.roll(row, 1, 1)), 1.0, 0.0)
        rank_row = jnp.dot(start.astype(jnp.bfloat16), upto, preferred_element_type=jnp.float32)[:1] - 1.0 + used
        begun = jnp.where(since, start[:1], 0.0).astype(jnp.bfloat16)
        rank_col = jnp.dot(begun, ones, preferred_element_type=jnp.float32)
        mine = (slot == rank_row) & (start[:1] > 0.0)
        ids = ids + jnp.sum(jnp.where(mine, row[:1] + 1.0, 0.0), axis=1, keepdims=True)
        slot_of.append(rank_col - 1.0 + used)
        used = used + rank_col[LANES - 1 :]
    differ = jnp.zeros((1, 1), jnp.float32)
    for band in range(bands):
        rows = patch[band * BAND : (band + 1) * BAND]
        uneven = jnp.max((rows != rows[:1]).astype(jnp.float32), axis=0, keepdims=True)
        differ = jnp.maximum(differ, jnp.max(uneven, axis=1, keepdims=True))
    slot_id = jnp.broadcast_to(ids - 1.0, ids_out.shape)
    ids_out[...] = jnp.where(slot == float(FLAG_SLOT), -1.0 - differ, slot_id)
    ids_in[z] = ids_out[...]

    slot_lane = iota((LANES, LANES), 1).astype(jnp.float32)
    for side in range(2):
        for band in range(bands):
            begin = (side * bands + band) * LANES
            hit = slot_of[band] == slot_lane - float(side * RUN_SLOTS)
            place[begin : begin + LANES] = hit.astype(jnp.float32).astype(jnp.bfloat16)

    def rim_copy(which, target):
        return pltpu.make_async_remote_copy(
            src_ref=rim_out.at[which], dst_ref=rim_in.at[which],
            send_sem=rim_sem.at[0, which], recv_sem=rim_sem.at[1, which],
            device_id=target, device_id_type=MESH_ID,
        )

    def ids_copy(peer, source):
        return pltpu.make_async_remote_copy(
            src_ref=ids_out, dst_ref=ids_in.at[source],
            send_sem=ids_sem.at[0, peer], recv_sem=ids_sem.at[1, source],
            device_id=at_z(peer), device_id_type=MESH_ID,
        )

    def gather_copy(part, peer, source):
        span = pl.ds(pair_start[part], len(PARTS[part]))
        return pltpu.make_async_remote_copy(
            src_ref=rows_out.at[span], dst_ref=rows_in.at[source, span],
            send_sem=gather_sem.at[0, part, peer], recv_sem=gather_sem.at[1, part, source],
            device_id=at_z(peer), device_id_type=MESH_ID,
        )

    def sum_copy(part, peer, source):
        span = pl.ds(pair_start[part], len(PARTS[part]))
        return pltpu.make_async_remote_copy(
            src_ref=sums_out.at[peer, span], dst_ref=sums_in.at[source, span],
            send_sem=sum_sem.at[0, part, peer], recv_sem=sum_sem.at[1, part, source],
            device_id=at_target(peer), device_id_type=MESH_ID,
        )

    pair_start = [sum(len(part) for part in PARTS[:i]) for i in range(len(PARTS))]
    z_peers = [((z + k) % n_z, (z + n_z - k) % n_z) for k in range(1, n_z)]
    plane_peers = [((me + k) % targets, (me + targets - k) % targets) for k in range(1, targets)]

    pl.semaphore_wait(barrier, len(senders))
    rims = [rim_copy(0, towards(1, 0)), rim_copy(1, towards(0, 1))]
    for copy in rims:
        copy.start()
    for peer, source in z_peers:
        ids_copy(peer, z).start()

    loads[4].wait()
    lift[...] = lift_t[...].T
    lower = lower_modes()
    table = group_table()
    lower_all = jnp.concatenate([lower] * VARS, axis=0)
    lower_all_16 = lower_all.astype(jnp.bfloat16)

    def flag_row(row):
        return (order[row : row + 1] == DEG - 1).astype(jnp.float32)

    def stage_values(b):
        keep = jnp.concatenate(
            [jnp.maximum(lower_all_16, flag_row(b * ROWS + i).astype(jnp.bfloat16)) for i in range(ROWS)], axis=1
        )
        values[b] = st[b].reshape(kmax, width) * keep

    def stage_faces(b):
        ta_b = ta[:, b * ROWS : (b + 1) * ROWS, :].reshape(face_len, width)
        if b == 0:
            before = rim_in[0]
        else:
            before = ta[:, b * ROWS - 1, :]
        tr_b = flat_r[:, b * width : (b + 1) * width]
        rim = rim_in[1].astype(jnp.float32)
        pieces = []
        for i in range(ROWS):
            moved = pltpu.roll(tr_b[:, i * LANES : (i + 1) * LANES].astype(jnp.float32), 1, 1)
            row = b * ROWS + i
            edge = pltpu.roll(rim, (LANES - row) % LANES, 1)
            pieces.append(jnp.where(lane == 0, jnp.where(rad > 0, edge, 0.0), moved).astype(jnp.bfloat16))
        faces[b, 0:face_len] = ta_b
        faces[b, face_len : 2 * face_len] = jnp.concatenate([before, ta_b[:, : width - LANES]], axis=1)
        faces[b, 2 * face_len : 3 * face_len] = tr_b
        faces[b, 3 * face_len :] = jnp.concatenate(pieces, axis=1)

    def weigh(part, b, residual):
        start, count = spans[part]
        adjoint = jnp.dot(lift[start : start + count], faces[b], preferred_element_type=jnp.float32)
        low = lower_all[start : start + count]
        total = None
        for i in range(ROWS):
            cut = slice(i * LANES, (i + 1) * LANES)
            term = adjoint[:, cut] * residual[:, cut] * jnp.maximum(low, flag_row(b * ROWS + i))
            total = term if total is None else total + term
        return total

    def residual_of(part, b):
        start, count = spans[part]
        return jnp.dot(jac[start : start + count], values[b], preferred_element_type=jnp.float32)

    def add_block(part, b, total):
        start, count = spans[part]
        band = b * ROWS // BAND
        if b * ROWS % BAND == 0:
            acc[band, start : start + count] = total
        else:
            acc[band, start : start + count] += total

    grouped = {}

    def group_band(part, band):
        members = [var for pair in PARTS[part] for var in pair]
        halves_of = []
        for var in members:
            halves_of += float_halves(acc[band, var * MODES : (var + 1) * MODES])
        both = jnp.concatenate(halves_of, axis=1).astype(jnp.bfloat16)
        sums = jnp.dot(table, both, preferred_element_type=jnp.float32)
        for i, var in enumerate(members):
            at = 2 * i * LANES
            grouped[var, band] = sums[:, at : at + LANES] + sums[:, at + LANES : at + 2 * LANES]

    def send_rows(part):
        for p, pair in enumerate(PARTS[part], pair_start[part]):
            terms = [grouped[var, band] for var in pair for band in range(bands)]
            rows_out[p] = table_dot(jnp.concatenate(terms, axis=1), place[: len(terms) * LANES])
        for peer, source in z_peers:
            gather_copy(part, peer, z).start()
        span = pl.ds(pair_start[part], len(PARTS[part]))
        rows_in[z, span] = rows_out[span]

    def send_sums(part):
        for peer, source in z_peers:
            gather_copy(part, peer, source).wait_recv()
        flags = [ids_in[peer, FLAG_SLOT : FLAG_SLOT + 1] for peer in range(n_z)]
        flag = -1.0 - functools.reduce(jnp.minimum, flags)
        held = range(pair_start[part], pair_start[part] + len(PARTS[part]))
        terms = [jnp.concatenate([rows_in[peer, p] for peer in range(n_z)], axis=1) for p in held]
        sums = table_dot(jnp.concatenate(terms, axis=0), choose[...])
        for i, p in enumerate(held):
            for target in range(targets):
                piece = sums[i * GROUP_ROWS : (i + 1) * GROUP_ROWS, target * LANES : (target + 1) * LANES]
                if p == 0:
                    piece = jnp.where(iota(piece.shape, 0) == GROUP_ROWS - 1, flag, piece)
                sums_out[target, p] = piece
        for peer, source in plane_peers:
            sum_copy(part, peer, me).start()
        span = pl.ds(pair_start[part], len(PARTS[part]))
        sums_in[me, span] = sums_out[me, span]

    def make_choose():
        for peer, source in z_peers:
            ids_copy(peer, source).wait_recv()
        here = iota((1, LANES), 1)
        sides = []
        for side in range(2):
            inside = (here >= side * PATCH_DEV) & (here < (side + 1) * PATCH_DEV)
            sides.append(jnp.where(inside, here - side * PATCH_DEV, -(2**20)).astype(jnp.float32))
        base = (z * targets * PATCH_DEV).astype(jnp.float32)
        for peer in range(n_z):
            for side in range(2):
                begin = (2 * peer + side) * RUN_SLOTS
                for target in range(targets):
                    hit = ids_in[peer] == sides[side] + (base + float(target * PATCH_DEV))
                    choose[begin : begin + RUN_SLOTS, target * LANES : (target + 1) * LANES] = hit.astype(
                        jnp.float32
                    ).astype(jnp.bfloat16)

    state_loads[0].wait()
    for copy in state_loads[1:] + jac_loads[1:]:
        copy.start()
    stage_values(0)
    jac_loads[0].wait()
    first = residual_of(0, 0)
    state_loads[1].wait()
    stage_values(1)
    second = residual_of(0, 1)
    for copy in rims:
        copy.wait_recv()
    for b in range(blocks):
        if b > 1:
            state_loads[b].wait()
            stage_values(b)
        stage_faces(b)
        residual = (first, second)[b] if b < 2 else residual_of(0, b)
        add_block(0, b, weigh(0, b, residual))
        if (b + 1) * ROWS % BAND == 0:
            group_band(0, b * ROWS // BAND)
    send_rows(0)
    jac_loads[1].wait()
    for b in range(blocks):
        add_block(1, b, weigh(1, b, residual_of(1, b)))
        if (b + 1) * ROWS % BAND == 0:
            group_band(1, b * ROWS // BAND)
        if b == 0:
            make_choose()
        if b == min(1, blocks - 1):
            send_sums(0)
    send_rows(1)
    send_sums(1)
    columns = []
    for part, pairs in enumerate(PARTS):
        for peer, source in plane_peers:
            sum_copy(part, peer, source).wait_recv()
        span = slice(pair_start[part], pair_start[part] + len(pairs))
        total = functools.reduce(jnp.add, [sums_in[source, span] for source in range(targets)])
        total = jnp.abs(total).reshape(len(pairs) * GROUP_ROWS, LANES)
        if part == 0:
            flag_ref[0, 0] = jnp.where(jnp.max(total[GROUP_ROWS - 1 : GROUP_ROWS]) > 0.0, 1, 0)
        pad = jnp.zeros((LANES - len(pairs) * GROUP_ROWS, LANES), jnp.float32)
        turned = jnp.concatenate([total, pad], axis=0).T
        for p, pair in enumerate(pairs):
            for side in range(len(pair)):
                columns.append(
                    turned[side * PATCH_DEV : (side + 1) * PATCH_DEV, p * GROUP_ROWS : p * GROUP_ROWS + PER_VAR]
                )
    out_ref[...] = jnp.concatenate(columns, axis=1)

    for copy in rims:
        copy.wait_send()
    for peer, source in z_peers:
        ids_copy(peer, z).wait_send()
    for part in range(len(PARTS)):
        for peer, source in z_peers:
            gather_copy(part, peer, z).wait_send()
        for peer, source in plane_peers:
            sum_copy(part, peer, me).wait_send()


def per_device(trace_azimuth, trace_radial, state, jacobian, lift_map, order, patch):
    face_len, rows_azi, rows_rad = trace_azimuth.shape
    kmax = jacobian.shape[0]
    n_azi, n_rad = lax.axis_size("azi"), lax.axis_size("rad")
    n_seat = SEATS if n_azi % SEATS == 0 else 1
    n_z, targets = n_azi // n_seat, n_seat * n_rad
    blocks = rows_azi // ROWS
    width = ROWS * LANES
    pairs = sum(len(part) for part in PARTS)
    f32, b16 = jnp.float32, jnp.bfloat16
    out, uneven = pl.pallas_call(
        functools.partial(fused_kernel, n_z, n_seat, n_rad),
        out_shape=(jax.ShapeDtypeStruct((PATCH_DEV, GROUPS), f32), jax.ShapeDtypeStruct((1, 1), jnp.int32)),
        in_specs=[pl.BlockSpec(memory_space=pl.ANY)] * 7,
        out_specs=(pl.BlockSpec(memory_space=pltpu.VMEM), pl.BlockSpec(memory_space=pltpu.SMEM)),
        scratch_shapes=[
            pltpu.VMEM(trace_azimuth.shape, b16),
            pltpu.VMEM(trace_radial.shape, b16),
            pltpu.VMEM((blocks, kmax, ROWS, LANES), b16),
            pltpu.VMEM(jacobian.shape, b16),
            pltpu.VMEM(lift_map.shape[::-1], b16),
            pltpu.VMEM(lift_map.shape, b16),
            pltpu.VMEM(order.shape, jnp.int32),
            pltpu.VMEM(patch.shape, jnp.int32),
            pltpu.VMEM((blocks, kmax, width), b16),
            pltpu.VMEM((blocks, 4 * face_len, width), b16),
            pltpu.VMEM((rows_azi // BAND, kmax, LANES), f32),
            pltpu.VMEM((face_len, rows_azi * LANES), b16),
            pltpu.VMEM((2, face_len, LANES), b16),
            pltpu.VMEM((2, face_len, LANES), b16),
            pltpu.VMEM((RUN_SLOTS, LANES), f32),
            pltpu.VMEM((n_z, RUN_SLOTS, LANES), f32),
            pltpu.VMEM((rows_azi // BAND * 2 * LANES, LANES), b16),
            pltpu.VMEM((n_z * 2 * RUN_SLOTS, targets * LANES), b16),
            pltpu.VMEM((pairs, GROUP_ROWS, LANES), f32),
            pltpu.VMEM((n_z, pairs, GROUP_ROWS, LANES), f32),
            pltpu.VMEM((targets, pairs, GROUP_ROWS, LANES), f32),
            pltpu.VMEM((targets, pairs, GROUP_ROWS, LANES), f32),
            pltpu.SemaphoreType.DMA((5 + len(PARTS),)),
            pltpu.SemaphoreType.DMA((blocks,)),
            pltpu.SemaphoreType.DMA((2, 2)),
            pltpu.SemaphoreType.DMA((2, n_z)),
            pltpu.SemaphoreType.DMA((2, len(PARTS), n_z)),
            pltpu.SemaphoreType.DMA((2, len(PARTS), targets)),
        ],
        compiler_params=pltpu.CompilerParams(collective_id=0, has_side_effects=True, vmem_limit_bytes=VLIM),
        cost_estimate=pl.CostEstimate(
            flops=2 * kmax * (kmax + 4 * face_len) * rows_azi * rows_rad,
            bytes_accessed=2 * kmax * rows_azi * rows_rad, transcendentals=0,
        ),
    )(trace_azimuth, trace_radial, state, jacobian, lift_map.T, order, patch)
    arguments = (trace_azimuth, trace_radial, state, jacobian, lift_map, order, patch)
    return lax.cond(uneven[0, 0] != 0, general_path, lambda *unused: out, *arguments)


def solution(mesh):
    in_specs = (
        P(None, "azi", "rad"),
        P(None, "azi", "rad"),
        P(None, "azi", "rad"),
        P(),
        P(),
        P("azi", "rad"),
        P("azi", "rad"),
    )
    out_specs = P(("azi", "rad"), None)
    return jax.shard_map(
        per_device, mesh=mesh, in_specs=in_specs, out_specs=out_specs, check_vma=False
    )
```
